256 devices in a mesh: dp: 32 (over z, y), block: 8 (over x, core).
Axes of the slice: x: 4, y: 4, z: 8, core: 2. Of those that a mesh axis runs over, the one named last changes fastest.
Arguments:
- x_act: bfloat16 [8, 16384, 4096], P('block', 'dp')
- g_out: bfloat16 [8, 16384, 4096], P('block', 'dp')
- proj_in: bfloat16 [8, 4096, 64], P('block'), may hold values from -0.09375 to 0.09375
- proj_out: bfloat16 [8, 4096, 64], P('block'), may hold values from -0.09375 to 0.09375
- queries: bfloat16 [8, 2048, 4096], P('block', 'dp'), may hold values from -6 to 6
- cand_ids: int32 [32, 32, 2], P('dp'), may hold values from 0 to 15, as said below
- cand_counts: int32 [32, 32], P('dp'), may hold values from 0 to 2, as said below
Outputs:
- scores: float32 [2048, 128], P(('dp', 'block'))
The draws below stay inside these ranges and needn't reach their ends.
Inputs may be any that keep to these rules, and one draw needn't show every extreme that they name: `cand_ids`: each list of a training shard d for an owner p names 2 distinct query blocks of p; slots at or past cand_counts[d, p] are padding. Every training shard d has cand_counts[d, d] = 2.
All inputs are finite; a program needn't handle non-finite values.
Results may differ from the reference program's by a relative error of at most 0.0096.
Values may be sent and summed in bfloat16 or wider, within the bound.
No kernel may reach another device: no remote copies, remote signals or barrier semaphores. Data moves between devices by JAX's collectives and lax.ppermute only.
A program may use at most 64 MiB of HBM per device.

```python
import math
import jax
import jax.numpy as jnp
from jax import lax

D = 4096
R = 64
E_DEV = 4
SEQ = 128
Q_DEV = 64
QB = 4
CAP = 2
LAYERS = 8
TRAIN = 128
TOKENS = 16384
QUERIES = 2048
QBO = 16


def draw_stream(key, salt):
    stream_key = jax.random.fold_in(key, salt)
    subkeys = jax.random.split(stream_key, 12)
    shape = (LAYERS, TOKENS, D)
    rising = 1.0 + 2.0 * jnp.arange(TOKENS, dtype=jnp.float32) / max(TOKENS - 1, 1)
    rising = rising[None, :, None]
    noise = jax.random.normal(subkeys[0], shape, jnp.float32)
    row_scale = jnp.ones((LAYERS, TOKENS, 1), jnp.float32)
    shared = jnp.zeros(shape, jnp.float32)
    for component in range(4):
        token_coef = jax.random.normal(subkeys[2 + 2 * component], (LAYERS, TOKENS, 1), jnp.float32)
        feature_dir = jax.random.normal(subkeys[3 + 2 * component], (LAYERS, 1, D), jnp.float32)
        shared = shared + token_coef * feature_dir
    return (rising * row_scale * (noise + shared)).astype(jnp.bfloat16)


def draw_x_act(key, part):
    return draw_stream(key, 101)


def draw_g_out(key, part):
    return draw_stream(key, 202)


def candidate_tables(key):
    owners = QUERIES // Q_DEV
    perm_keys = jax.random.split(jax.random.fold_in(key, 7), owners * owners)
    perms = jax.vmap(lambda subkey: jax.random.permutation(subkey, QBO))(perm_keys)
    id_table = perms[:, :CAP].reshape(owners, owners, CAP).astype(jnp.int32)
    base_count = jax.random.randint(jax.random.fold_in(key, 11), (owners, owners), 0, CAP + 1)
    heat = jax.random.randint(jax.random.fold_in(key, 13), (1, owners), 0, 3)
    counts = jnp.clip(base_count + heat - 1, 0, CAP)
    counts = jnp.where(jnp.eye(owners, dtype=bool), CAP, counts).astype(jnp.int32)
    return (id_table, counts)


def draw_cand_ids(key, part):
    return candidate_tables(key)[0]


def draw_cand_counts(key, part):
    return candidate_tables(key)[1]


def shard_levels(key, shape, cuts, least, largest):
    factor_of = 1.0
    for dim, parts in cuts:
        heights = jax.random.uniform(jax.random.fold_in(jax.random.fold_in(key, 6), dim), (parts,), jnp.float32, least / len(cuts), largest / len(cuts))
        factor_of = factor_of * jnp.repeat(jnp.exp(heights), shape[dim] // parts).reshape((-1,) + (1,) * (len(shape) - 1 - dim))
    return factor_of


def centred(key, dims, scale, most, cuts=(), kind=jnp.bfloat16):
    level = shard_levels(key, dims, cuts, -0.22, 0.18) if cuts else 1.0
    values = jax.random.normal(key, dims, jnp.float32) * scale * level
    return jnp.minimum(jnp.maximum(values, -most), most).astype(kind)


def setup_inputs(seed: int = 0) -> dict:
    arg_keys = jax.random.split(jax.random.key(seed), 8)
    return {
        "x_act": draw_x_act(jax.random.fold_in(arg_keys[7], 71), 0),
        "g_out": draw_g_out(jax.random.fold_in(arg_keys[7], 71), 0),
        "proj_in": centred(arg_keys[2], (LAYERS, D, R), D ** -0.5, 0.09375, ((0, 8),)),
        "proj_out": centred(arg_keys[3], (LAYERS, D, R), D ** -0.5, 0.09375, ((0, 8),)),
        "queries": centred(arg_keys[4], (LAYERS, QUERIES, R * R), 1.0, 6.0, ((0, 8), (1, 32))),
        "cand_ids": draw_cand_ids(jax.random.fold_in(arg_keys[7], 71), 0),
        "cand_counts": draw_cand_counts(jax.random.fold_in(arg_keys[7], 71), 0),
    }


DAMP = 0.1

def kron_inverse(factor):
    width = factor.shape[0]
    identity = jnp.eye(width, dtype=jnp.float32)
    damping = DAMP * jnp.trace(factor) / width + 1e-06
    lower_factor = jnp.linalg.cholesky(factor + damping * identity)
    return jax.scipy.linalg.cho_solve((lower_factor, True), identity)

def reference(x_act, g_out, proj_in, proj_out, queries, cand_ids, cand_counts):
    score_sum = jnp.zeros((QUERIES, TRAIN), jnp.float32)
    for layer_idx in range(LAYERS):
        act_proj = jnp.dot(x_act[layer_idx].astype(jnp.float32), proj_in[layer_idx].astype(jnp.float32), preferred_element_type=jnp.float32).astype(jnp.bfloat16)
        grad_proj = jnp.dot(g_out[layer_idx].astype(jnp.float32), proj_out[layer_idx].astype(jnp.float32), preferred_element_type=jnp.float32).astype(jnp.bfloat16)
        factor_a = jnp.dot(act_proj.T.astype(jnp.float32), act_proj.astype(jnp.float32), preferred_element_type=jnp.float32) / TOKENS
        factor_g = jnp.dot(grad_proj.T.astype(jnp.float32), grad_proj.astype(jnp.float32), preferred_element_type=jnp.float32) / TOKENS
        inverse_a = kron_inverse(factor_a)
        inverse_g = kron_inverse(factor_g)
        act_three = act_proj.astype(jnp.float32).reshape(TRAIN, SEQ, R)
        grad_three = grad_proj.astype(jnp.float32).reshape(TRAIN, SEQ, R)
        example_grad = jnp.einsum('esi,esj->eij', grad_three, act_three, precision=lax.Precision.HIGHEST) / SEQ
        left_side = jnp.einsum('ij,ejk->eik', inverse_g, example_grad, precision=lax.Precision.HIGHEST)
        precond = jnp.einsum('eik,kl->eil', left_side, inverse_a, precision=lax.Precision.HIGHEST)
        precond = precond.reshape(TRAIN, R * R).astype(jnp.bfloat16)
        score_sum = score_sum + lax.dot_general(queries[layer_idx].astype(jnp.float32), precond.astype(jnp.float32), (((1,), (1,)), ((), ())), preferred_element_type=jnp.float32)
    owners = QUERIES // Q_DEV
    slot_live = jnp.arange(CAP)[None, None, :] < cand_counts[:, :, None]
    matches = (cand_ids[:, :, :, None] == jnp.arange(QBO)[None, None, None, :]) & slot_live[:, :, :, None]
    live = jnp.any(matches, axis=2).astype(jnp.float32)
    mask_blocks = jnp.transpose(live, (1, 2, 0))
    mask = jnp.broadcast_to(mask_blocks[:, :, None, :, None], (owners, QBO, QB, owners, E_DEV)).reshape(QUERIES, TRAIN)
    scale = 1.0 / math.sqrt(R * R * LAYERS)
    return score_sum * scale * mask
```

```python
import jax
import jax.numpy as jnp
from jax import lax
from jax.sharding import PartitionSpec as P

E_DEV = 4
SEQ = 128
QB = 4
CAP = 2
Z = 8
Y = 4
F16 = jnp.float16
F32 = jnp.float32
BF16 = jnp.bfloat16
DAMP = 0.1
HI = lax.Precision.HIGHEST

Z_GROUPS = [[z * Y + y for z in range(Z)] for y in range(Y)]
Y_GROUPS = [[z * Y + y for y in range(Y)] for z in range(Z)]


def y_shift(k):
    return [(z * Y + y, z * Y + (y + k) % Y) for z in range(Z) for y in range(Y)]


def spread(x, n):
    return jnp.broadcast_to(x[None], (n,) + x.shape)


def exponent(m):
    return jnp.clip(jnp.floor(jnp.log2(jnp.maximum(m, 1e-30))), -96.0, 96.0)


def kron_inverse(factor):
    width = factor.shape[0]
    identity = jnp.eye(width, dtype=F32)
    damping = DAMP * jnp.trace(factor) / width + 1e-06
    lower_factor = jnp.linalg.cholesky(factor + damping * identity)
    return jax.scipy.linalg.cho_solve((lower_factor, True), identity)


def body(x_act, g_out, proj_in, proj_out, queries, cand_ids, cand_counts):
    width = proj_in.shape[2]
    n_owners = lax.axis_size("dp")
    n_layers = lax.axis_size("block")
    me = lax.axis_index("dp")
    my_y = me % Y
    act = jnp.dot(x_act[0], proj_in[0], preferred_element_type=F32).astype(BF16)
    grad = jnp.dot(g_out[0], proj_out[0], preferred_element_type=F32).astype(BF16)
    rows = (((0,), (0,)), ((), ()))
    part_a = lax.dot_general(act, act, rows, preferred_element_type=F32)
    part_g = lax.dot_general(grad, grad, rows, preferred_element_type=F32)
    example = jnp.einsum(
        "esi,esj->eij",
        grad.reshape(E_DEV, SEQ, width),
        act.reshape(E_DEV, SEQ, width),
        preferred_element_type=F32,
    ) / SEQ

    e_exp = exponent(jnp.max(jnp.abs(example), axis=(1, 2)))
    small = (example * (4096.0 * jnp.exp2(-e_exp))[:, None, None]).astype(F16)
    small = small.reshape(128, 128)
    a_exp = exponent(jnp.max(jnp.diagonal(part_a)))
    g_exp = exponent(jnp.max(jnp.diagonal(part_g)))
    parts = jnp.concatenate(
        [part_a * (256.0 * jnp.exp2(-a_exp)), part_g * (256.0 * jnp.exp2(-g_exp))], axis=1
    )
    high = parts.astype(F16)
    low = ((parts - high.astype(F32)) * 2048.0).astype(F16)
    live_slot = jnp.arange(CAP)[None, :] < cand_counts[0][:, None]
    ids = jnp.where(live_slot, cand_ids[0], 99).reshape(n_owners * CAP).astype(F32)
    meta = jnp.concatenate([ids, e_exp, jnp.stack([a_exp, g_exp]), jnp.zeros((58,), F32)])
    meta = jnp.broadcast_to(meta.astype(F16)[None], (16, 128))
    packet = jnp.concatenate([small, meta, high, low], axis=0)

    got = lax.all_to_all(
        spread(packet, Z), "dp", 0, 0, axis_index_groups=Z_GROUPS, tiled=True
    )
    mine = got[:, :144]
    got_meta = got[:, 128, :].astype(F32)
    lane_exp = jnp.where(
        jnp.arange(128)[None, :] < width, got_meta[:, 68:69], got_meta[:, 69:70]
    )
    lane_scale = (jnp.exp2(lane_exp) / 256.0)[:, None, :]
    both = got[:, 144:208].astype(F32) + got[:, 208:272].astype(F32) * (1.0 / 2048.0)
    sums = jnp.sum(both * lane_scale, axis=0)
    sums = jnp.sum(
        lax.all_to_all(spread(sums, Y), "dp", 0, 0, axis_index_groups=Y_GROUPS, tiled=True), axis=0
    )
    token_total = x_act.shape[1] * n_owners
    factors = jnp.stack([sums[:, :width], sums[:, width:]]) / token_total
    inverses = jax.vmap(kron_inverse)(factors)

    gathered = jnp.stack([mine] + [lax.ppermute(mine, "dp", y_shift(k)) for k in range(1, Y)])
    gathered = gathered.reshape(n_owners, 144, 128)
    train = gathered[:, :128].reshape(n_owners * E_DEV, width * width).astype(F32)
    notes = gathered[:, 128].astype(F32)

    query = queries[0].astype(F32).reshape(-1, width, width)
    owned = query.shape[0]
    query = jnp.einsum("qij,jk->qik", query, inverses[0], precision=HI)
    query = jnp.einsum("ij,qjk->qik", inverses[1], query, precision=HI)
    query = query.reshape(owned, width * width)
    dense = lax.dot_general(
        query, train, (((1,), (1,)), ((), ())), precision=HI, preferred_element_type=F32
    )
    slots = lax.dynamic_slice(notes, (0, me * CAP), (n_owners, CAP))
    blocks = (jnp.arange(owned) // QB).astype(F32)
    live = jnp.any(slots[None] == blocks[:, None, None], axis=2)
    scale = 1.0 / float(width * width * n_layers) ** 0.5
    column = jnp.exp2(notes[:, 64:68]) * (scale / 4096.0)
    scores = jnp.where(live[:, :, None], dense.reshape(owned, n_owners, E_DEV) * column[None], 0.0)
    scores = scores.reshape(owned, Y, Z, E_DEV)
    back = jnp.stack([scores[:, (-m) % Y] for m in range(Y)] * 2, axis=1)
    scores = lax.dynamic_slice_in_dim(back, (Y - my_y) % Y, Y, axis=1)
    scores = jnp.swapaxes(scores, 1, 2).reshape(n_layers, owned // n_layers, n_owners * E_DEV)
    return jnp.sum(lax.all_to_all(scores, "block", 0, 0, tiled=True), axis=0)


def solution(mesh):
    return jax.shard_map(
        body,
        mesh=mesh,
        in_specs=(
            P("block", "dp", None),
            P("block", "dp", None),
            P("block", None, None),
            P("block", None, None),
            P("block", "dp", None),
            P("dp", None, None),
            P("dp", None),
        ),
        out_specs=P(("dp", "block"), None),
        check_vma=False,
    )
```

```python
import jax
import jax.numpy as jnp
from jax import lax
from jax.experimental import pallas as pl
from jax.experimental.pallas import tpu as pltpu
from jax.sharding import Mesh
from jax.sharding import PartitionSpec as P

E_DEV = 4
SEQ = 128
QB = 4
CAP = 2
Z = 8
Y = 4
R = 64
LANES = 128
ROWS = E_DEV * SEQ
D = 4096
F16 = jnp.float16
F32 = jnp.float32
BF16 = jnp.bfloat16
DAMP = 0.1
NT = (((1,), (1,)), ((), ()))
NN = (((1,), (0,)), ((), ()))
CHUNKS = 8
WIDTH = D // CHUNKS
MIB = 1024 * 1024

HIGH = 128
LOW = 168
NAMED = 208
PACK = 216


def dot(a, b, dims):
    return lax.dot_general(a, b, dims, preferred_element_type=F32)


def lane_iota(rows):
    return lax.broadcasted_iota(jnp.int32, (rows, LANES), 1)


def row_iota(rows):
    return lax.broadcasted_iota(jnp.int32, (rows, LANES), 0)


def swap_halves(x):
    return pltpu.roll(x, R, 1)


def exponent(m):
    return jnp.clip(jnp.floor(jnp.log2(jnp.maximum(m, 1e-30))), -96.0, 96.0)


def split(x):
    high = x.astype(BF16)
    return high, (x - high.astype(F32)).astype(BF16)


def project_kernel(
    x_hbm, g_hbm, pin_hbm, pout_hbm, me_ref, ids_ref, counts_ref, out_ref, x, g, pin, pout, acc, sem
):
    copies = []

    def fetch(src, dst):
        copy = pltpu.make_async_copy(src, dst, sem.at[len(copies)])
        copy.start()
        copies.append(copy)
        return copy

    pin_copy = fetch(pin_hbm, pin)
    x_copies, g_copies = [], []
    for c in range(CHUNKS):
        cols = slice(c * WIDTH, (c + 1) * WIDTH)
        x_copies.append(fetch(x_hbm.at[:, cols], x.at[:, cols]))
        if c == 0:
            pout_copy = fetch(pout_hbm, pout)
        g_copies.append(fetch(g_hbm.at[:, cols], g.at[:, cols]))

    own = lane_iota(1) // E_DEV == me_ref[0]
    for owner in range(Z * Y):
        for slot in range(CAP):
            block = jnp.where(slot < counts_ref[0, owner], ids_ref[slot, owner], 99)
            row = NAMED + owner % Y * CAP + slot
            out_ref[owner // Y, row : row + 1, :] = jnp.where(own, block, 0).astype(F32)

    pin_copy.wait()
    for c in range(CHUNKS):
        cols = slice(c * WIDTH, (c + 1) * WIDTH)
        x_copies[c].wait()
        xp = dot(pin[:, cols], x[:, cols], NT)
        if c == 0:
            pout_copy.wait()
        g_copies[c].wait()
        gp = dot(pout[:, cols], g[:, cols], NT)
        if c == 0:
            acc[:R] = xp
            acc[R:] = gp
        else:
            acc[:R] += xp
            acc[R:] += gp

    first = lane_iota(R) < R
    both = acc[...].astype(BF16)
    total = jnp.zeros((LANES, LANES), F32)
    powers = jnp.zeros((1, LANES), F32)
    lanes = lane_iota(1)
    examples = []
    for e in range(E_DEV):
        cols = both[:, e * SEQ : (e + 1) * SEQ]
        gram = dot(cols, cols, NT)
        total = total + gram
        example = gram[R:] * (1.0 / SEQ)
        peak = jnp.max(jnp.where(first, jnp.abs(example), 0.0), axis=(0, 1), keepdims=True)
        power = exponent(peak)
        examples.append(example * (4096.0 * jnp.exp2(-power)))
        powers = jnp.where(lanes == me_ref[0] * E_DEV + e, power, powers)
    pairs = [
        jnp.where(first, examples[0], swap_halves(examples[1])),
        jnp.where(first, examples[2], swap_halves(examples[3])),
    ]
    parts = jnp.where(first, total[:R], total[R:])
    on_diag = row_iota(R) == lane_iota(R) % R
    diag = jnp.where(on_diag, parts, 0.0)
    power_a = exponent(jnp.max(jnp.where(first, diag, 0.0), axis=(0, 1), keepdims=True))
    power_g = exponent(jnp.max(jnp.where(first, 0.0, diag), axis=(0, 1), keepdims=True))
    parts = parts * (128.0 * jnp.exp2(-jnp.where(lanes < R, power_a, power_g)))
    other = swap_halves(parts)
    mixed = jnp.where(lane_iota(R) >= row_iota(R), parts, other)
    packed = jnp.where(first[:32], mixed[:32], swap_halves(mixed[32:]))
    diag = jnp.sum(jnp.where(on_diag & first, other, 0.0), axis=0, keepdims=True)
    packed_high = jnp.round(packed * 2.0) * 0.5
    diag_high = jnp.round(diag * 2.0) * 0.5
    rows = row_iota(8)

    def tail(a, b, c, d):
        return jnp.where(
            rows == 0, a, jnp.where(rows == 1, b, jnp.where(rows == 2, c, jnp.where(rows == 3, d, 0.0)))
        )

    high_tail = tail(diag_high, power_a, power_g, powers)
    low_tail = tail((diag - diag_high) * 1024.0, 0.0, 0.0, 0.0)
    packed_low = (packed - packed_high) * 1024.0
    for z in range(Z):
        out_ref[z, 0:64, :] = pairs[0]
        out_ref[z, 64:128, :] = pairs[1]
        out_ref[z, HIGH : HIGH + 32, :] = packed_high
        out_ref[z, HIGH + 32 : LOW, :] = high_tail
        out_ref[z, LOW : LOW + 32, :] = packed_low
        out_ref[z, LOW + 32 : NAMED, :] = low_tail


def project(x, g, pin, pout, me, ids, counts):
    hbm = pl.BlockSpec(memory_space=pl.ANY)
    smem = pl.BlockSpec(memory_space=pltpu.SMEM)
    return pl.pallas_call(
        project_kernel,
        out_shape=jax.ShapeDtypeStruct((Z, PACK, LANES), F32),
        in_specs=[hbm, hbm, hbm, hbm, smem, smem, smem],
        out_specs=pl.BlockSpec(memory_space=pltpu.VMEM),
        scratch_shapes=[
            pltpu.VMEM((ROWS, D), BF16),
            pltpu.VMEM((ROWS, D), BF16),
            pltpu.VMEM((R, D), BF16),
            pltpu.VMEM((R, D), BF16),
            pltpu.VMEM((LANES, ROWS), F32),
            pltpu.SemaphoreType.DMA((2 + 2 * CHUNKS,)),
        ],
        compiler_params=pltpu.CompilerParams(vmem_limit_bytes=60 * MIB),
        name="project",
    )(x, g, pin, pout, me, ids, counts)


def invert_pair(m):
    lanes = lane_iota(R)
    rows = row_iota(R)
    half = jnp.where(lanes < R, 0, R)
    local = lane_iota(1) % R
    for k in range(0, R, 2):
        c0 = jnp.take_along_axis(m, half + k, axis=1)
        c1 = jnp.take_along_axis(m, half + (k + 1), axis=1)
        r0 = m[k : k + 1]
        r1 = m[k + 1 : k + 2]
        p00 = c0[k : k + 1]
        p10 = c0[k + 1 : k + 2]
        p01 = c1[k : k + 1]
        p11 = c1[k + 1 : k + 2]
        inv = 1.0 / (p00 * p11 - p01 * p10)
        is0 = local == k
        is1 = local == k + 1
        r0 = jnp.where(is0, 1.0, jnp.where(is1, 0.0, r0))
        r1 = jnp.where(is1, 1.0, jnp.where(is0, 0.0, r1))
        q0 = (p11 * r0 - p01 * r1) * inv
        q1 = (p00 * r1 - p10 * r0) * inv
        kept = jnp.where(is0 | is1, 0.0, m)
        m = kept - c0 * q0 - c1 * q1
        m = jnp.where(rows == k, q0, jnp.where(rows == k + 1, q1, m))
    return m


def block_diagonal(a):
    wide = jnp.concatenate([a, a], axis=1)
    tall = jnp.concatenate([wide, wide, wide, wide], axis=0)
    r = lax.broadcasted_iota(jnp.int32, (4 * R, 4 * R), 0) // R
    c = lax.broadcasted_iota(jnp.int32, (4 * R, 4 * R), 1) // R
    return jnp.where(r == c, tall, 0.0)


def score_kernel(tokens, scale, parts_ref, t_ref, info_ref, y_ref, *refs):
    queries, out_ref, lh, ll, u, tp = refs[:Y], *refs[Y:]
    total = jnp.sum(parts_ref[...], axis=0)
    first = lane_iota(R) < R
    row, col = row_iota(R), lane_iota(R) % R
    packed = total[:32]
    moved = swap_halves(packed)
    mixed = jnp.concatenate(
        [jnp.where(first[:32], packed, moved), jnp.where(first[:32], moved, packed)], axis=0
    )
    turned = jnp.concatenate([mixed, mixed], axis=0).T[:R]
    diag_g = total[32:33]
    diag_g = jnp.where(first[:1], diag_g, swap_halves(diag_g))
    factor_a = jnp.where(col >= row, mixed, turned)
    factor_g = jnp.where(col < row, mixed, jnp.where(col > row, turned, diag_g))
    m = jnp.where(first, factor_a, factor_g) * (1.0 / tokens)
    on_diag = row == col
    diag = jnp.sum(jnp.where(on_diag, m, 0.0), axis=0, keepdims=True)
    trace_a = jnp.sum(jnp.where(first[:1], diag, 0.0), axis=1, keepdims=True)
    trace_g = jnp.sum(jnp.where(first[:1], 0.0, diag), axis=1, keepdims=True)
    damp = (DAMP / R) * jnp.where(first[:1], trace_a, trace_g) + 1e-06
    m = invert_pair(jnp.where(on_diag, m + damp, m))
    other = swap_halves(m)
    ia = block_diagonal(jnp.where(first, m, other))
    ig = jnp.where(first, other, m)[:, :R]

    g0 = ig.astype(BF16)
    g1, g2 = split(ig - g0.astype(F32))
    left = jnp.concatenate([g0, g1, g2], axis=0)
    for z in range(Z):
        block = t_ref[z]
        th, tl = split(jnp.concatenate([block[:R], block[R:]], axis=1))
        p = dot(left, th, NN)
        q = dot(left[: 2 * R], tl, NN)
        high, low = split(p[:R] + ((p[R : 2 * R] + q[:R]) + (p[2 * R :] + q[R:])))
        lh[z * R : (z + 1) * R, :] = high
        ll[z * R : (z + 1) * R, :] = low
    ah, al = split(ia)
    for c in range(2):
        rows = slice(c * 256, (c + 1) * 256)
        high = lh[rows, :]
        p = dot(high, ah, NN) + (dot(ll[rows, :], ah, NN) + dot(high, al, NN))
        for s in range(4):
            for t in range(2):
                pair = (c * 4 + s) * 2 + t
                u[pair * R : (pair + 1) * R, :] = p[s * R : (s + 1) * R, t * 128 : (t + 1) * 128]
    low_half = first[:16]
    for i in range(0, R, 2):
        w0 = u[pl.ds(i, 16, stride=R), :]
        w1 = u[pl.ds(i + 1, 16, stride=R), :]
        cols = slice(i * R, (i + 2) * R)
        tp[0:16, cols] = jnp.where(low_half, w0, swap_halves(w1)).astype(BF16)
        tp[16:32, cols] = jnp.where(low_half, swap_halves(w0), w1).astype(BF16)

    my_y = y_ref[0]
    s = jnp.concatenate([dot(queries[k][...], tp[...], NT) for k in range(Y)], axis=0)
    take = row_iota(32)
    place = take % 16 // 2 * (Y * E_DEV) + my_y * E_DEV + take % 2 * 2 + take // 16
    onehot = jnp.where(place == lane_iota(32), 1.0, 0.0).astype(BF16)
    s0 = s.astype(BF16)
    s1, s2 = split(s - s0.astype(F32))
    s = dot(s0, onehot, NN) + (dot(s1, onehot, NN) + dot(s2, onehot, NN))
    column = jnp.exp2(info_ref[8:9, :]) * scale
    blocks = (row // QB).astype(F32)
    for k in range(Y):
        owner = (my_y + Y - k) % Y
        id0, id1 = info_ref[0:1, :], info_ref[1:2, :]
        for y in range(1, Y):
            id0 = jnp.where(owner == y, info_ref[2 * y : 2 * y + 1, :], id0)
            id1 = jnp.where(owner == y, info_ref[2 * y + 1 : 2 * y + 2, :], id1)
        live = (blocks == id0) | (blocks == id1)
        out_ref[owner] = jnp.where(live, s[k * R : (k + 1) * R] * column, 0.0)


def score(parts, train, info, y, queries, tokens, scale):
    vmem = pl.BlockSpec(memory_space=pltpu.VMEM)
    smem = pl.BlockSpec(memory_space=pltpu.SMEM)
    return pl.pallas_call(
        lambda *refs: score_kernel(float(tokens), scale, *refs),
        out_shape=jax.ShapeDtypeStruct((Y, R, LANES), F32),
        in_specs=[vmem, vmem, vmem, smem] + [vmem] * Y,
        out_specs=vmem,
        scratch_shapes=[
            pltpu.VMEM((Z * R, 256), BF16),
            pltpu.VMEM((Z * R, 256), BF16),
            pltpu.VMEM((2 * Z * R, LANES), F32),
            pltpu.VMEM((Z * E_DEV, D), BF16),
        ],
        compiler_params=pltpu.CompilerParams(vmem_limit_bytes=32 * MIB),
        name="score",
    )(parts, train, info, y, *queries)


def body(x_act, g_out, proj_in, proj_out, queries, cand_ids, cand_counts):
    n_layers = lax.axis_size("block")
    my_y = lax.axis_index("y").astype(jnp.int32)
    me = lax.axis_index("z").astype(jnp.int32) * Y + my_y
    query = [queries[0]]
    for k in range(1, Y):
        query.append(lax.ppermute(queries[0], "y", [(y, (y + k) % Y) for y in range(Y)]))
    packet = project(
        x_act[0],
        g_out[0],
        proj_in[0].T,
        proj_out[0].T,
        jnp.reshape(me, (1,)),
        cand_ids[0].T,
        cand_counts,
    )
    got = lax.all_to_all(packet.astype(F16), "z", 0, 0, tiled=True)

    r = jnp.arange(40)[:, None]
    lane = jnp.arange(LANES)[None, :]
    upper = (lane % R >= r + R // 2 * (lane // R)) & (r < 32)
    power = jnp.where(
        upper[None],
        got[:, HIGH + 33 : HIGH + 34].astype(F32),
        got[:, HIGH + 34 : HIGH + 35].astype(F32),
    )
    both = got[:, HIGH:LOW].astype(F32) + got[:, LOW:NAMED].astype(F32) * (1.0 / 1024.0)
    sums = jnp.sum(both * (jnp.exp2(power) * (1.0 / 128.0)), axis=0)
    spread = jnp.broadcast_to(sums[None], (Y,) + sums.shape)
    spread, got = lax.optimization_barrier((spread, got))
    parts = lax.all_to_all(spread, "y", 0, 0, tiled=True)

    train = got[:, :128].astype(F32)
    info = jnp.concatenate(
        [
            jnp.sum(got[:, NAMED:].astype(F32), axis=0),
            jnp.sum(got[:, HIGH + 35 : HIGH + 43].astype(F32), axis=0),
        ],
        axis=0,
    )
    scale = 1.0 / float(R * R * n_layers) ** 0.5 / 4096.0
    tokens = ROWS * Z * Y
    scores = score(parts, train, info, jnp.reshape(my_y, (1,)), query, tokens, scale)
    scores = scores.reshape(Y * n_layers, R // n_layers, LANES)
    return jnp.sum(lax.all_to_all(scores, ("y", "block"), 0, 0, tiled=True), axis=0)


def solution(mesh):
    split_mesh = Mesh(mesh.devices.reshape(Z, Y, -1), ("z", "y", "block"))
    shard = ("z", "y")
    return jax.shard_map(
        body,
        mesh=split_mesh,
        in_specs=(
            P("block", shard, None),
            P("block", shard, None),
            P("block", None, None),
            P("block", None, None),
            P("block", shard, None),
            P(shard, None, None),
            P(shard, None),
        ),
        out_specs=P(("z", "y", "block"), None),
        check_vma=False,
    )
```

```python
import jax
import jax.numpy as jnp
from jax import lax
from jax.experimental import pallas as pl
from jax.experimental.pallas import tpu as pltpu
from jax.sharding import Mesh
from jax.sharding import PartitionSpec as P

E_DEV = 4
SEQ = 128
QB = 4
CAP = 2
Z = 8
Y = 4
R = 64
LANES = 128
ROWS = E_DEV * SEQ
D = 4096
F16 = jnp.float16
F32 = jnp.float32
BF16 = jnp.bfloat16
DAMP = 0.1
NT = (((1,), (1,)), ((), ()))
NN = (((1,), (0,)), ((), ()))
TN = (((0,), (0,)), ((), ()))
CHUNKS = 8
WIDTH = D // CHUNKS
MIB = 1024 * 1024

HIGH = 128
NOTES = 160
LOW = 168
PACK = 200


def dot(a, b, dims):
    return lax.dot_general(a, b, dims, preferred_element_type=F32)


def lane_iota(rows):
    return lax.broadcasted_iota(jnp.int32, (rows, LANES), 1)


def row_iota(rows):
    return lax.broadcasted_iota(jnp.int32, (rows, LANES), 0)


def swap_halves(x):
    return pltpu.roll(x, R, 1)


def exponent(m):
    return jnp.clip(jnp.floor(jnp.log2(jnp.maximum(m, 1e-30))), -96.0, 96.0)


def split(x):
    high = x.astype(BF16)
    return high, (x - high.astype(F32)).astype(BF16)


def project_kernel(
    x_hbm, g_hbm, pin_hbm, pout_hbm, me_ref, ids_ref, counts_ref, out_ref, x, g, pin, pout, acc, sem
):
    copies = []

    def fetch(src, dst):
        copy = pltpu.make_async_copy(src, dst, sem.at[len(copies)])
        copy.start()
        copies.append(copy)
        return copy

    pin_copy = fetch(pin_hbm, pin)
    x_copies, g_copies = [], []
    for c in range(CHUNKS):
        cols = slice(c * WIDTH, (c + 1) * WIDTH)
        x_copies.append(fetch(x_hbm.at[:, cols], x.at[:, cols]))
        if c == 0:
            pout_copy = fetch(pout_hbm, pout)
        g_copies.append(fetch(g_hbm.at[:, cols], g.at[:, cols]))

    lanes = lane_iota(1)
    named = jnp.zeros((1, LANES), jnp.int32)
    for owner in range(Z * Y):
        for slot in range(CAP):
            block = jnp.where(slot < counts_ref[0, owner], ids_ref[slot, owner], 99)
            named = jnp.where(lanes == owner * CAP + slot, block, named)

    pin_copy.wait()
    for c in range(CHUNKS):
        cols = slice(c * WIDTH, (c + 1) * WIDTH)
        x_copies[c].wait()
        xp = dot(pin[:, cols], x[:, cols], NT)
        if c == 0:
            pout_copy.wait()
        g_copies[c].wait()
        gp = dot(pout[:, cols], g[:, cols], NT)
        if c == 0:
            acc[:R] = xp
            acc[R:] = gp
        else:
            acc[:R] += xp
            acc[R:] += gp

    first = lane_iota(R) < R
    both = acc[...].astype(BF16)
    on_diag = row_iota(R) == lane_iota(R) % R
    total = jnp.zeros((LANES, LANES), F32)
    examples, peaks = [], []
    for e in range(E_DEV):
        cols = both[:, e * SEQ : (e + 1) * SEQ]
        gram = dot(cols, cols, NT)
        total = total + gram
        example = jnp.where(first, gram[R:], 0.0) * (1.0 / SEQ)
        examples.append(example)
        peaks.append(jnp.max(jnp.abs(example), axis=0, keepdims=True))
    parts = jnp.where(first, total[:R], total[R:])
    diag = jnp.max(jnp.where(on_diag, parts, 0.0), axis=0, keepdims=True)
    peaks.append(jnp.where(first[:1], diag, 0.0))
    peaks.append(jnp.where(first[:1], 0.0, diag))
    peaks.append(jnp.zeros((2, LANES), F32))
    power = exponent(jnp.max(jnp.concatenate(peaks, axis=0), axis=1, keepdims=True))
    grow = 4096.0 * jnp.exp2(-power)
    powers = jnp.zeros((1, LANES), F32)
    for e in range(E_DEV):
        examples[e] = examples[e] * grow[e : e + 1]
        powers = jnp.where(lanes == me_ref[0] * E_DEV + e, power[e : e + 1], powers)
    out_ref[0:64, :] = jnp.where(first, examples[0], swap_halves(examples[1]))
    out_ref[64:128, :] = jnp.where(first, examples[2], swap_halves(examples[3]))
    parts = parts * (jnp.where(lanes < R, grow[4:5], grow[5:6]) * (1.0 / 32.0))
    other = swap_halves(parts)
    mixed = jnp.where(lane_iota(R) >= row_iota(R), parts, other)
    packed = jnp.where(first[:32], mixed[:32], swap_halves(mixed[32:]))
    diag = jnp.sum(jnp.where(on_diag, jnp.where(first, other, parts), 0.0), axis=0, keepdims=True)
    high = jnp.round(packed * 2.0) * 0.5
    diag_high = jnp.round(diag * 2.0) * 0.5
    diag = jnp.where(first[:1], diag_high, (diag - diag_high) * 1024.0)
    rows = row_iota(8)
    notes = jnp.zeros((8, LANES), F32)
    for i, line in enumerate([diag, power[4:5], power[5:6], powers, named.astype(F32)]):
        notes = jnp.where(rows == i, line, notes)
    out_ref[HIGH:NOTES, :] = high
    out_ref[NOTES:LOW, :] = notes
    out_ref[LOW:PACK, :] = (packed - high) * 1024.0


def project(x, g, pin, pout, me, ids, counts):
    hbm = pl.BlockSpec(memory_space=pl.ANY)
    smem = pl.BlockSpec(memory_space=pltpu.SMEM)
    return pl.pallas_call(
        project_kernel,
        out_shape=jax.ShapeDtypeStruct((PACK, LANES), F32),
        in_specs=[hbm, hbm, hbm, hbm, smem, smem, smem],
        out_specs=pl.BlockSpec(memory_space=pltpu.VMEM),
        scratch_shapes=[
            pltpu.VMEM((ROWS, D), BF16),
            pltpu.VMEM((ROWS, D), BF16),
            pltpu.VMEM((R, D), BF16),
            pltpu.VMEM((R, D), BF16),
            pltpu.VMEM((LANES, ROWS), F32),
            pltpu.SemaphoreType.DMA((2 + 2 * CHUNKS,)),
        ],
        compiler_params=pltpu.CompilerParams(vmem_limit_bytes=60 * MIB),
        name="project",
    )(x, g, pin, pout, me, ids, counts)


def invert_pair(m):
    lanes = lane_iota(R)
    rows = row_iota(R)
    half = jnp.where(lanes < R, 0, R)
    local = lane_iota(1) % R
    for k in range(0, R, 2):
        c0 = jnp.take_along_axis(m, half + k, axis=1)
        c1 = jnp.take_along_axis(m, half + (k + 1), axis=1)
        r0 = m[k : k + 1]
        r1 = m[k + 1 : k + 2]
        p00 = c0[k : k + 1]
        p10 = c0[k + 1 : k + 2]
        p01 = c1[k : k + 1]
        p11 = c1[k + 1 : k + 2]
        inv = 1.0 / (p00 * p11 - p01 * p10)
        is0 = local == k
        is1 = local == k + 1
        r0 = jnp.where(is0, 1.0, jnp.where(is1, 0.0, r0))
        r1 = jnp.where(is1, 1.0, jnp.where(is0, 0.0, r1))
        q0 = (p11 * r0 - p01 * r1) * inv
        q1 = (p00 * r1 - p10 * r0) * inv
        kept = jnp.where(is0 | is1, 0.0, m)
        m = kept - c0 * q0 - c1 * q1
        m = jnp.where(rows == k, q0, jnp.where(rows == k + 1, q1, m))
    return m


def block_diagonal(a):
    wide = jnp.concatenate([a, a], axis=1)
    tall = jnp.concatenate([wide, wide, wide, wide], axis=0)
    r = lax.broadcasted_iota(jnp.int32, (4 * R, 4 * R), 0) // R
    c = lax.broadcasted_iota(jnp.int32, (4 * R, 4 * R), 1) // R
    return jnp.where(r == c, tall, 0.0)


def solve_kernel(tokens, p0, p1, p2, p3, t_ref, tp, lh, ll, u):
    total = (p0[...] + p2[...]) + (p1[...] + p3[...])
    first = lane_iota(R) < R
    row, col = row_iota(R), lane_iota(R) % R
    packed = total[:32]
    moved = swap_halves(packed)
    mixed = jnp.concatenate(
        [jnp.where(first[:32], packed, moved), jnp.where(first[:32], moved, packed)], axis=0
    )
    turned = jnp.concatenate([mixed, mixed], axis=0).T[:R]
    diag_g = total[32:33]
    moved = swap_halves(diag_g)
    diag_g = jnp.where(first[:1], diag_g, moved) + jnp.where(first[:1], moved, diag_g) * (1.0 / 1024.0)
    factor_a = jnp.where(col >= row, mixed, turned)
    factor_g = jnp.where(col < row, mixed, jnp.where(col > row, turned, diag_g))
    m = jnp.where(first, factor_a, factor_g) * (1.0 / tokens)
    on_diag = row == col
    diag = jnp.sum(jnp.where(on_diag, m, 0.0), axis=0, keepdims=True)
    trace_a = jnp.sum(jnp.where(first[:1], diag, 0.0), axis=1, keepdims=True)
    trace_g = jnp.sum(jnp.where(first[:1], 0.0, diag), axis=1, keepdims=True)
    damp = (DAMP / R) * jnp.where(first[:1], trace_a, trace_g) + 1e-06
    m = invert_pair(jnp.where(on_diag, m + damp, m))
    other = swap_halves(m)
    ia = block_diagonal(jnp.where(first, m, other))
    ig = jnp.where(first, other, m)[:, :R]

    g0 = ig.astype(BF16)
    g1, g2 = split(ig - g0.astype(F32))
    left = jnp.concatenate([g0, g1, g2], axis=0)
    for z in range(Z):
        th, tl = split(jnp.concatenate([t_ref[z, :R, :], t_ref[z, R : 2 * R, :]], axis=1))
        p = dot(left, th, NN)
        q = dot(left[: 2 * R], tl, NN)
        high, low = split(p[:R] + ((p[R : 2 * R] + q[:R]) + (p[2 * R :] + q[R:])))
        lh[z * R : (z + 1) * R, :] = high
        ll[z * R : (z + 1) * R, :] = low
    ah, al = split(ia)
    for c in range(2):
        rows = slice(c * 256, (c + 1) * 256)
        high = lh[rows, :]
        p = dot(high, ah, NN) + (dot(ll[rows, :], ah, NN) + dot(high, al, NN))
        for s in range(4):
            for t in range(2):
                pair = (c * 4 + s) * 2 + t
                u[pair * R : (pair + 1) * R, :] = p[s * R : (s + 1) * R, t * 128 : (t + 1) * 128]
    low_half = first[:16]
    for i in range(0, R, 2):
        w0 = u[pl.ds(i, 16, stride=R), :]
        w1 = u[pl.ds(i + 1, 16, stride=R), :]
        cols = slice(i * R, (i + 2) * R)
        tp[0:16, cols] = jnp.where(low_half, w0, swap_halves(w1)).astype(BF16)
        tp[16:32, cols] = jnp.where(low_half, swap_halves(w0), w1).astype(BF16)


def score_kernel(scale, tp, got_ref, at_ref, *refs):
    queries, out_ref, names = refs[: Y + 1], *refs[Y + 1 :]
    my_z, my_y = at_ref[0], at_ref[1]
    s = jnp.concatenate([dot(queries[k][...], tp[...], NT) for k in range(Y + 1)], axis=0)
    take = row_iota(32)
    place = take % 16 // 2 * (Y * E_DEV) + my_y * E_DEV + take % 2 * 2 + take // 16
    onehot = jnp.where(place == lane_iota(32), 1.0, 0.0).astype(BF16)
    s0 = s.astype(BF16)
    s1, s2 = split(s - s0.astype(F32))
    s = dot(s0, onehot, NN) + (dot(s1, onehot, NN) + dot(s2, onehot, NN))
    lanes = lane_iota(2 * Z)
    mine = (lanes // (Y * E_DEV) == row_iota(2 * Z)) & (lanes // E_DEV % Y == my_y)
    power = jnp.zeros((1, LANES), F32)
    listed = []
    for z in range(Z):
        power = power + got_ref[z, NOTES + 3 : NOTES + 4, :]
        listed.append(got_ref[z, NOTES + 4 : NOTES + 5, :])
    listed = jnp.concatenate(listed + [jnp.zeros((Z, LANES), F32)], axis=0).astype(BF16)
    names[...] = dot(listed, jnp.where(mine, 1.0, 0.0).astype(BF16), TN)
    named = names[pl.ds(pl.multiple_of(my_z * (Y * CAP), Y * CAP), Y * CAP), :]
    column = jnp.exp2(power) * scale
    blocks = (row_iota(R) // QB).astype(F32)
    for k in range(Y):
        owner = (my_y + Y - k) % Y
        id0, id1 = named[0:1], named[1:2]
        for y in range(1, Y):
            id0 = jnp.where(owner == y, named[2 * y : 2 * y + 1], id0)
            id1 = jnp.where(owner == y, named[2 * y + 1 : 2 * y + 2], id1)
        live = (blocks == id0) | (blocks == id1)
        out_ref[owner] = jnp.where(live, s[k * R : (k + 1) * R] * column, 0.0)


def solve(parts, train, tokens):
    vmem = pl.BlockSpec(memory_space=pltpu.VMEM)
    return pl.pallas_call(
        lambda *refs: solve_kernel(float(tokens), *refs),
        out_shape=jax.ShapeDtypeStruct((Z * E_DEV, D), BF16),
        in_specs=[vmem] * (Y + 1),
        out_specs=vmem,
        scratch_shapes=[
            pltpu.VMEM((Z * R, 256), BF16),
            pltpu.VMEM((Z * R, 256), BF16),
            pltpu.VMEM((2 * Z * R, LANES), F32),
        ],
        compiler_params=pltpu.CompilerParams(vmem_limit_bytes=32 * MIB),
        cost_estimate=pl.CostEstimate(flops=4 * 10**9, bytes_accessed=2 * MIB, transcendentals=0),
        name="solve",
    )(*parts, train)


def score(tp, got, at, queries, scale):
    vmem = pl.BlockSpec(memory_space=pltpu.VMEM)
    smem = pl.BlockSpec(memory_space=pltpu.SMEM)
    return pl.pallas_call(
        lambda *refs: score_kernel(scale, *refs),
        out_shape=jax.ShapeDtypeStruct((Y, R, LANES), F32),
        in_specs=[vmem, vmem, smem] + [vmem] * (Y + 1),
        out_specs=vmem,
        scratch_shapes=[pltpu.VMEM((LANES, LANES), F32)],
        compiler_params=pltpu.CompilerParams(vmem_limit_bytes=32 * MIB),
        cost_estimate=pl.CostEstimate(flops=10**9, bytes_accessed=3 * MIB, transcendentals=0),
        name="score",
    )(tp, got, at, *queries)


def body(x_act, g_out, proj_in, proj_out, queries, cand_ids, cand_counts):
    n_layers = lax.axis_size("block")
    my_y = lax.axis_index("y").astype(jnp.int32)
    my_z = lax.axis_index("z").astype(jnp.int32)
    me = my_z * Y + my_y
    up = [(y, (y + 1) % Y) for y in range(Y)]
    down = [(y, (y - 1) % Y) for y in range(Y)]
    below = lax.ppermute(queries[0], "y", up)
    above = lax.ppermute(queries[0], "y", down)
    packet = project(
        x_act[0],
        g_out[0],
        proj_in[0].T,
        proj_out[0].T,
        jnp.reshape(me, (1,)),
        cand_ids[0].T,
        cand_counts,
    )
    packet = jnp.broadcast_to(packet.astype(F16)[None], (Z, PACK, LANES))
    got = lax.all_to_all(packet, "z", 0, 0, tiled=True)

    r = jnp.arange(40)[:, None]
    lane = jnp.arange(LANES)[None, :]
    upper = (lane % R >= r + R // 2 * (lane // R)) & (r < 32)
    power = jnp.where(
        upper[None],
        got[:, NOTES + 1 : NOTES + 2].astype(F32),
        got[:, NOTES + 2 : NOTES + 3].astype(F32),
    )
    low = jnp.pad(got[:, LOW:].astype(F32), ((0, 0), (0, LOW - NOTES), (0, 0)))
    both = got[:, HIGH:LOW].astype(F32) + low * (1.0 / 1024.0)
    sums = jnp.sum(both * (jnp.exp2(power) * (1.0 / 128.0)), axis=0)
    parts = [sums] + [
        lax.ppermute(sums, "y", [(y, (y + k) % Y) for y in range(Y)]) for k in range(1, Y)
    ]
    sums, got, below, above = lax.optimization_barrier((sums, got, below, above))
    half = queries.shape[1] // 2
    across_low = lax.ppermute(below[:half], "y", up)
    across_high = lax.ppermute(above[half:], "y", down)
    query = [queries[0], below, across_low, across_high, above]

    wide = got[:, :LOW].astype(F32)
    scale = 1.0 / float(R * R * n_layers) ** 0.5 / 4096.0
    tokens = ROWS * Z * Y
    precond = solve(parts, wide, tokens)
    scores = score(precond, wide, jnp.stack([my_z, my_y]), query, scale)
    scores = scores.reshape(Y * n_layers, R // n_layers, LANES)
    return jnp.sum(lax.all_to_all(scores, ("y", "block"), 0, 0, tiled=True), axis=0)


def solution(mesh):
    split_mesh = Mesh(mesh.devices.reshape(Z, Y, -1), ("z", "y", "block"))
    shard = ("z", "y")
    return jax.shard_map(
        body,
        mesh=split_mesh,
        in_specs=(
            P("block", shard, None),
            P("block", shard, None),
            P("block", None, None),
            P("block", None, None),
            P("block", shard, None),
            P(shard, None, None),
            P(shard, None),
        ),
        out_specs=P(("z", "y", "block"), None),
        check_vma=False,
    )
```

```python
import jax
import jax.numpy as jnp
from jax import lax
from jax.experimental import pallas as pl
from jax.experimental.pallas import tpu as pltpu
from jax.sharding import Mesh
from jax.sharding import PartitionSpec as P

E_DEV = 4
SEQ = 128
QB = 4
CAP = 2
Z = 8
Y = 4
R = 64
LANES = 128
ROWS = E_DEV * SEQ
D = 4096
F16 = jnp.float16
F32 = jnp.float32
BF16 = jnp.bfloat16
DAMP = 0.1
NT = (((1,), (1,)), ((), ()))
NN = (((1,), (0,)), ((), ()))
TN = (((0,), (0,)), ((), ()))
CHUNKS = 8
WIDTH = D // CHUNKS
MIB = 1024 * 1024

NOTES = 128
HIGH = 136
LOW = 168
PACK = 200


def dot(a, b, dims):
    return lax.dot_general(a, b, dims, preferred_element_type=F32)


def lane_iota(rows):
    return lax.broadcasted_iota(jnp.int32, (rows, LANES), 1)


def row_iota(rows):
    return lax.broadcasted_iota(jnp.int32, (rows, LANES), 0)


def swap_halves(x):
    return pltpu.roll(x, R, 1)


def exponent(m):
    return jnp.clip(jnp.floor(jnp.log2(jnp.maximum(m, 1e-30))), -96.0, 96.0)


def split(x):
    high = x.astype(BF16)
    return high, (x - high.astype(F32)).astype(BF16)


def project_kernel(
    x_hbm, g_hbm, pin_hbm, pout_hbm, me_ref, ids_ref, counts_ref, out_ref, x, g, pin, pout, acc, sem
):
    copies = []

    def fetch(src, dst):
        copy = pltpu.make_async_copy(src, dst, sem.at[len(copies)])
        copy.start()
        copies.append(copy)
        return copy

    pin_copy = fetch(pin_hbm, pin)
    x_copies, g_copies = [], []
    for c in range(CHUNKS):
        cols = slice(c * WIDTH, (c + 1) * WIDTH)
        x_copies.append(fetch(x_hbm.at[:, cols], x.at[:, cols]))
        if c == 0:
            pout_copy = fetch(pout_hbm, pout)
        g_copies.append(fetch(g_hbm.at[:, cols], g.at[:, cols]))

    lanes = lane_iota(1)
    named = jnp.zeros((1, LANES), jnp.int32)
    for owner in range(Z * Y):
        for slot in range(CAP):
            block = jnp.where(slot < counts_ref[0, owner], ids_ref[slot, owner], 99)
            named = jnp.where(lanes == owner * CAP + slot, block, named)

    pin_copy.wait()
    for c in range(CHUNKS):
        cols = slice(c * WIDTH, (c + 1) * WIDTH)
        x_copies[c].wait()
        xp = dot(pin[:, cols], x[:, cols], NT)
        if c == 0:
            pout_copy.wait()
        g_copies[c].wait()
        gp = dot(pout[:, cols], g[:, cols], NT)
        if c == 0:
            acc[:R] = xp
            acc[R:] = gp
        else:
            acc[:R] += xp
            acc[R:] += gp

    first = lane_iota(R) < R
    both = acc[...].astype(BF16)
    on_diag = row_iota(R) == lane_iota(R) % R
    total = jnp.zeros((LANES, LANES), F32)
    examples, peaks = [], []
    for e in range(E_DEV):
        cols = both[:, e * SEQ : (e + 1) * SEQ]
        gram = dot(cols, cols, NT)
        total = total + gram
        example = jnp.where(first, gram[R:], 0.0) * (1.0 / SEQ)
        examples.append(example)
        peaks.append(jnp.max(jnp.abs(example), axis=0, keepdims=True))
    parts = jnp.where(first, total[:R], total[R:])
    diag = jnp.max(jnp.where(on_diag, parts, 0.0), axis=0, keepdims=True)
    peaks.append(jnp.where(first[:1], diag, 0.0))
    peaks.append(jnp.where(first[:1], 0.0, diag))
    peaks.append(jnp.zeros((2, LANES), F32))
    power = exponent(jnp.max(jnp.concatenate(peaks, axis=0), axis=1, keepdims=True))
    grow = 4096.0 * jnp.exp2(-power)
    powers = jnp.zeros((1, LANES), F32)
    for e in range(E_DEV):
        examples[e] = examples[e] * grow[e : e + 1]
        powers = jnp.where(lanes == me_ref[0] * E_DEV + e, power[e : e + 1], powers)
    out_ref[0:64, :] = jnp.where(first, examples[0], swap_halves(examples[1]))
    out_ref[64:128, :] = jnp.where(first, examples[2], swap_halves(examples[3]))
    parts = parts * (jnp.where(lanes < R, grow[4:5], grow[5:6]) * (1.0 / 32.0))
    other = swap_halves(parts)
    mixed = jnp.where(lane_iota(R) >= row_iota(R), parts, other)
    packed = jnp.where(first[:32], mixed[:32], swap_halves(mixed[32:]))
    diag = jnp.sum(jnp.where(on_diag, jnp.where(first, other, parts), 0.0), axis=0, keepdims=True)
    high = jnp.round(packed * 2.0) * 0.5
    diag_high = jnp.round(diag * 2.0) * 0.5
    diag = jnp.where(first[:1], diag_high, (diag - diag_high) * 1024.0)
    rows = row_iota(8)
    notes = jnp.zeros((8, LANES), F32)
    for i, line in enumerate([diag, power[4:5], power[5:6], powers, named.astype(F32)]):
        notes = jnp.where(rows == i, line, notes)
    out_ref[NOTES:HIGH, :] = notes
    out_ref[HIGH:LOW, :] = high
    out_ref[LOW:PACK, :] = (packed - high) * 1024.0


def project(x, g, pin, pout, me, ids, counts):
    hbm = pl.BlockSpec(memory_space=pl.ANY)
    smem = pl.BlockSpec(memory_space=pltpu.SMEM)
    return pl.pallas_call(
        project_kernel,
        out_shape=jax.ShapeDtypeStruct((PACK, LANES), F32),
        in_specs=[hbm, hbm, hbm, hbm, smem, smem, smem],
        out_specs=pl.BlockSpec(memory_space=pltpu.VMEM),
        scratch_shapes=[
            pltpu.VMEM((ROWS, D), BF16),
            pltpu.VMEM((ROWS, D), BF16),
            pltpu.VMEM((R, D), BF16),
            pltpu.VMEM((R, D), BF16),
            pltpu.VMEM((LANES, ROWS), F32),
            pltpu.SemaphoreType.DMA((2 + 2 * CHUNKS,)),
        ],
        compiler_params=pltpu.CompilerParams(vmem_limit_bytes=60 * MIB),
        name="project",
    )(x, g, pin, pout, me, ids, counts)


def invert_pair(m):
    lanes = lane_iota(R)
    rows = row_iota(R)
    half = jnp.where(lanes < R, 0, R)
    local = lane_iota(1) % R
    for k in range(0, R, 2):
        c0 = jnp.take_along_axis(m, half + k, axis=1)
        c1 = jnp.take_along_axis(m, half + (k + 1), axis=1)
        r0 = m[k : k + 1]
        r1 = m[k + 1 : k + 2]
        p00 = c0[k : k + 1]
        p10 = c0[k + 1 : k + 2]
        p01 = c1[k : k + 1]
        p11 = c1[k + 1 : k + 2]
        inv = 1.0 / (p00 * p11 - p01 * p10)
        is0 = local == k
        is1 = local == k + 1
        r0 = jnp.where(is0, 1.0, jnp.where(is1, 0.0, r0))
        r1 = jnp.where(is1, 1.0, jnp.where(is0, 0.0, r1))
        q0 = (p11 * r0 - p01 * r1) * inv
        q1 = (p00 * r1 - p10 * r0) * inv
        kept = jnp.where(is0 | is1, 0.0, m)
        m = kept - c0 * q0 - c1 * q1
        m = jnp.where(rows == k, q0, jnp.where(rows == k + 1, q1, m))
    return m


def block_diagonal(a):
    wide = jnp.concatenate([a, a], axis=1)
    tall = jnp.concatenate([wide, wide, wide, wide], axis=0)
    r = lax.broadcasted_iota(jnp.int32, (4 * R, 4 * R), 0) // R
    c = lax.broadcasted_iota(jnp.int32, (4 * R, 4 * R), 1) // R
    return jnp.where(r == c, tall, 0.0)


def precondition(t_ref, left, ah, al, lh, ll, u, tp_ref):
    for z in range(Z):
        th, tl = split(jnp.concatenate([t_ref[z, :R, :], t_ref[z, R : 2 * R, :]], axis=1))
        p = dot(left, th, NN)
        q = dot(left[: 2 * R], tl, NN)
        high, low = split(p[:R] + ((p[R : 2 * R] + q[:R]) + (p[2 * R :] + q[R:])))
        lh[z * R : (z + 1) * R, :] = high
        ll[z * R : (z + 1) * R, :] = low
    for c in range(2):
        rows = slice(c * 256, (c + 1) * 256)
        high = lh[rows, :]
        p = dot(high, ah, NN) + (dot(ll[rows, :], ah, NN) + dot(high, al, NN))
        for s in range(4):
            for t in range(2):
                pair = (c * 4 + s) * 2 + t
                u[pair * R : (pair + 1) * R, :] = p[s * R : (s + 1) * R, t * 128 : (t + 1) * 128]
    low_half = lane_iota(16) < R
    for i in range(0, R, 2):
        w0 = u[pl.ds(i, 16, stride=R), :]
        w1 = u[pl.ds(i + 1, 16, stride=R), :]
        cols = slice(i * R, (i + 2) * R)
        tp_ref[0:16, cols] = jnp.where(low_half, w0, swap_halves(w1)).astype(BF16)
        tp_ref[16:32, cols] = jnp.where(low_half, swap_halves(w0), w1).astype(BF16)


def solve_kernel(tokens, p0, p1, p2, p3, t_ref, tp_ref, left_ref, ah_ref, al_ref, lh, ll, u):
    total = (p0[...] + p2[...]) + (p1[...] + p3[...])
    first = lane_iota(R) < R
    row, col = row_iota(R), lane_iota(R) % R
    packed = total[8:]
    moved = swap_halves(packed)
    mixed = jnp.concatenate(
        [jnp.where(first[:32], packed, moved), jnp.where(first[:32], moved, packed)], axis=0
    )
    turned = jnp.concatenate([mixed, mixed], axis=0).T[:R]
    diag_g = total[0:1]
    moved = swap_halves(diag_g)
    diag_g = jnp.where(first[:1], diag_g, moved) + jnp.where(first[:1], moved, diag_g) * (1.0 / 1024.0)
    factor_a = jnp.where(col >= row, mixed, turned)
    factor_g = jnp.where(col < row, mixed, jnp.where(col > row, turned, diag_g))
    m = jnp.where(first, factor_a, factor_g) * (1.0 / tokens)
    on_diag = row == col
    diag = jnp.sum(jnp.where(on_diag, m, 0.0), axis=0, keepdims=True)
    trace_a = jnp.sum(jnp.where(first[:1], diag, 0.0), axis=1, keepdims=True)
    trace_g = jnp.sum(jnp.where(first[:1], 0.0, diag), axis=1, keepdims=True)
    damp = (DAMP / R) * jnp.where(first[:1], trace_a, trace_g) + 1e-06
    m = invert_pair(jnp.where(on_diag, m + damp, m))
    other = swap_halves(m)
    ah, al = split(block_diagonal(jnp.where(first, m, other)))
    ig = jnp.where(first, other, m)[:, :R]
    g0 = ig.astype(BF16)
    g1, g2 = split(ig - g0.astype(F32))
    left = jnp.concatenate([g0, g1, g2], axis=0)
    left_ref[...] = left
    ah_ref[...] = ah
    al_ref[...] = al
    precondition(t_ref, left, ah, al, lh, ll, u, tp_ref)


def solve(parts, wide, tokens):
    vmem = pl.BlockSpec(memory_space=pltpu.VMEM)
    return pl.pallas_call(
        lambda *refs: solve_kernel(float(tokens), *refs),
        out_shape=(
            jax.ShapeDtypeStruct((Z * E_DEV, D), BF16),
            jax.ShapeDtypeStruct((3 * R, R), BF16),
            jax.ShapeDtypeStruct((4 * R, 4 * R), BF16),
            jax.ShapeDtypeStruct((4 * R, 4 * R), BF16),
        ),
        in_specs=[vmem] * (Y + 1),
        out_specs=(vmem,) * 4,
        scratch_shapes=[
            pltpu.VMEM((Z * R, 256), BF16),
            pltpu.VMEM((Z * R, 256), BF16),
            pltpu.VMEM((2 * Z * R, LANES), F32),
        ],
        compiler_params=pltpu.CompilerParams(vmem_limit_bytes=32 * MIB),
        cost_estimate=pl.CostEstimate(flops=4 * 10**9, bytes_accessed=2 * MIB, transcendentals=0),
        name="solve",
    )(*parts, wide)


def score_kernel(
    scale, tp, left_ref, ah_ref, al_ref, wide, far, at_ref, q0, q1, out_ref, lh, ll, u, tq, names
):
    my_z, my_y, far_y = at_ref[0], at_ref[1], at_ref[2]
    precondition(far, left_ref[...], ah_ref[...], al_ref[...], lh, ll, u, tq)
    lanes = lane_iota(2 * Z)
    rows = row_iota(2 * Z)
    source = jnp.where(rows < Z, my_y, far_y)
    mine = (lanes // (Y * E_DEV) == rows % Z) & (lanes // E_DEV % Y == source)
    power = jnp.zeros((1, LANES), F32)
    listed = []
    for ref in (wide, far):
        for z in range(Z):
            power = power + ref[z, NOTES + 3 : NOTES + 4, :]
            listed.append(ref[z, NOTES + 4 : NOTES + 5, :])
    listed = jnp.concatenate(listed, axis=0).astype(BF16)
    names[...] = dot(listed, jnp.where(mine, 1.0, 0.0).astype(BF16), TN)
    named = names[pl.ds(pl.multiple_of(my_z * (Y * CAP), Y * CAP), Y * CAP), :]
    column = jnp.exp2(power) * scale

    examples = jnp.concatenate([tp[...], tq[...]], axis=0)
    s = jnp.concatenate([dot(q0[...], examples, NT), dot(q1[...], examples, NT)], axis=0)
    take = row_iota(64)
    y = jnp.where(take < 32, my_y, far_y)
    take = take % 32
    place = take % 16 // 2 * (Y * E_DEV) + y * E_DEV + take % 2 * 2 + take // 16
    onehot = jnp.where(place == lane_iota(64), 1.0, 0.0).astype(BF16)
    s0 = s.astype(BF16)
    s1, s2 = split(s - s0.astype(F32))
    s = dot(s0, onehot, NN) + (dot(s1, onehot, NN) + dot(s2, onehot, NN))
    blocks = (row_iota(R) // QB).astype(F32)
    for k in range(2):
        owner = my_y if k == 0 else my_y + 1 - my_y % 2 * 2
        id0, id1 = named[0:1], named[1:2]
        for y in range(1, Y):
            id0 = jnp.where(owner == y, named[2 * y : 2 * y + 1], id0)
            id1 = jnp.where(owner == y, named[2 * y + 1 : 2 * y + 2], id1)
        live = (blocks == id0) | (blocks == id1)
        out_ref[owner % 2] = jnp.where(live, s[k * R : (k + 1) * R] * column, 0.0)


def score(solved, wide, far, at, queries, scale):
    vmem = pl.BlockSpec(memory_space=pltpu.VMEM)
    smem = pl.BlockSpec(memory_space=pltpu.SMEM)
    return pl.pallas_call(
        lambda *refs: score_kernel(scale, *refs),
        out_shape=jax.ShapeDtypeStruct((2, R, LANES), F32),
        in_specs=[vmem] * 6 + [smem] + [vmem] * 2,
        out_specs=vmem,
        scratch_shapes=[
            pltpu.VMEM((Z * R, 256), BF16),
            pltpu.VMEM((Z * R, 256), BF16),
            pltpu.VMEM((2 * Z * R, LANES), F32),
            pltpu.VMEM((Z * E_DEV, D), BF16),
            pltpu.VMEM((LANES, LANES), F32),
        ],
        compiler_params=pltpu.CompilerParams(vmem_limit_bytes=32 * MIB),
        cost_estimate=pl.CostEstimate(flops=10**9, bytes_accessed=3 * MIB, transcendentals=0),
        name="score",
    )(*solved, wide, far, at, *queries)


def body(x_act, g_out, proj_in, proj_out, queries, cand_ids, cand_counts):
    n_layers = lax.axis_size("block")
    my_z = lax.axis_index("z").astype(jnp.int32)
    my_y = lax.axis_index(("yh", "yl")).astype(jnp.int32)
    me = my_z * Y + my_y
    far_y = (my_y + 3 + my_y % 2 * 2) % Y
    near = lax.ppermute(queries[0], "yl", [(0, 1), (1, 0)])
    packet = project(
        x_act[0],
        g_out[0],
        proj_in[0].T,
        proj_out[0].T,
        jnp.reshape(me, (1,)),
        cand_ids[0].T,
        cand_counts,
    )
    packet = jnp.broadcast_to(packet.astype(F16)[None], (Z, PACK, LANES))
    got = lax.all_to_all(packet, "z", 0, 0, tiled=True)

    r = jnp.arange(LOW - NOTES)[:, None] - (HIGH - NOTES)
    lane = jnp.arange(LANES)[None, :]
    upper = (lane % R >= r + R // 2 * (lane // R)) & (r >= 0)
    power = jnp.where(
        upper[None],
        got[:, NOTES + 1 : NOTES + 2].astype(F32),
        got[:, NOTES + 2 : NOTES + 3].astype(F32),
    )
    low = jnp.pad(got[:, LOW:].astype(F32), ((0, 0), (HIGH - NOTES, 0), (0, 0)))
    both = got[:, NOTES:LOW].astype(F32) + low * (1.0 / 1024.0)
    sums = jnp.sum(both * (jnp.exp2(power) * (1.0 / 128.0)), axis=0)
    parts = [sums] + [
        lax.ppermute(sums, ("yh", "yl"), [(y, (y + k) % Y) for y in range(Y)]) for k in range(1, Y)
    ]
    sums, got = lax.optimization_barrier((sums, got))
    own = got[:, :HIGH]
    far = lax.ppermute(own, ("yh", "yl"), [(0, 3), (3, 0), (1, 2), (2, 1)])

    scale = 1.0 / float(R * R * n_layers) ** 0.5 / 4096.0
    wide = own.astype(F32)
    solved = solve(parts, wide, ROWS * Z * Y)
    at = jnp.stack([my_z, my_y, far_y])
    scores = score(solved, wide, far.astype(F32), at, [queries[0], near], scale)
    scores = scores.reshape(2 * n_layers, R // n_layers, LANES)
    return jnp.sum(lax.all_to_all(scores, ("yl", "block"), 0, 0, tiled=True), axis=0)


def solution(mesh):
    axes = ("z", "yh", "yl", "block")
    split_mesh = Mesh(mesh.devices.reshape(Z, 2, 2, -1), axes)
    shard = axes[:3]
    return jax.shard_map(
        body,
        mesh=split_mesh,
        in_specs=(
            P("block", shard, None),
            P("block", shard, None),
            P("block", None, None),
            P("block", None, None),
            P("block", shard, None),
            P(shard, None, None),
            P(shard, None),
        ),
        out_specs=P(axes, None),
        check_vma=False,
    )
```

```python
import jax
import jax.numpy as jnp
from jax import lax
from jax.experimental import pallas as pl
from jax.experimental.pallas import tpu as pltpu
from jax.sharding import Mesh
from jax.sharding import PartitionSpec as P

E_DEV = 4
SEQ = 128
QB = 4
CAP = 2
Z = 8
Y = 4
R = 64
LANES = 128
ROWS = E_DEV * SEQ
D = 4096
F16 = jnp.float16
F32 = jnp.float32
BF16 = jnp.bfloat16
DAMP = 0.1
NT = (((1,), (1,)), ((), ()))
NN = (((1,), (0,)), ((), ()))
TN = (((0,), (0,)), ((), ()))
CHUNKS = 8
WIDTH = D // CHUNKS
PANEL = 8
MIB = 1024 * 1024

NOTES = 128
HIGH = 136
LOW = 168
PACK = 200


def dot(a, b, dims):
    return lax.dot_general(a, b, dims, preferred_element_type=F32)


def lane_iota(rows):
    return lax.broadcasted_iota(jnp.int32, (rows, LANES), 1)


def row_iota(rows):
    return lax.broadcasted_iota(jnp.int32, (rows, LANES), 0)


def swap_halves(x):
    return pltpu.roll(x, R, 1)


def exponent(m):
    return jnp.clip(jnp.floor(jnp.log2(jnp.maximum(m, 1e-30))), -96.0, 96.0)


def split(x):
    high = x.astype(BF16)
    return high, (x - high.astype(F32)).astype(BF16)


def project_kernel(
    x_hbm, g_hbm, pin_hbm, pout_hbm, me_ref, ids_ref, counts_ref, out_ref, x, g, pin, pout, acc, sem
):
    copies = []

    def fetch(src, dst):
        copy = pltpu.make_async_copy(src, dst, sem.at[len(copies)])
        copy.start()
        copies.append(copy)
        return copy

    pin_copy = fetch(pin_hbm, pin)
    x_copies, g_copies = [], []
    for c in range(CHUNKS):
        cols = slice(c * WIDTH, (c + 1) * WIDTH)
        x_copies.append(fetch(x_hbm.at[:, cols], x.at[:, cols]))
        if c == 0:
            pout_copy = fetch(pout_hbm, pout)
        g_copies.append(fetch(g_hbm.at[:, cols], g.at[:, cols]))

    lanes = lane_iota(1)
    named = jnp.zeros((1, LANES), jnp.int32)
    for owner in range(Z * Y):
        for slot in range(CAP):
            block = jnp.where(slot < counts_ref[0, owner], ids_ref[slot, owner], 99)
            named = jnp.where(lanes == owner * CAP + slot, block, named)

    pin_copy.wait()
    for c in range(CHUNKS):
        cols = slice(c * WIDTH, (c + 1) * WIDTH)
        x_copies[c].wait()
        xp = dot(pin[:, cols], x[:, cols], NT)
        if c == 0:
            pout_copy.wait()
        g_copies[c].wait()
        gp = dot(pout[:, cols], g[:, cols], NT)
        if c == 0:
            acc[:R] = xp
            acc[R:] = gp
        else:
            acc[:R] += xp
            acc[R:] += gp

    first = lane_iota(R) < R
    both = acc[...].astype(BF16)
    on_diag = row_iota(R) == lane_iota(R) % R
    total = jnp.zeros((LANES, LANES), F32)
    examples, peaks = [], []
    for e in range(E_DEV):
        cols = both[:, e * SEQ : (e + 1) * SEQ]
        gram = dot(cols, cols, NT)
        total = total + gram
        example = jnp.where(first, gram[R:], 0.0) * (1.0 / SEQ)
        examples.append(example)
        peaks.append(jnp.max(jnp.abs(example), axis=0, keepdims=True))
    parts = jnp.where(first, total[:R], total[R:])
    diag = jnp.max(jnp.where(on_diag, parts, 0.0), axis=0, keepdims=True)
    peaks.append(jnp.where(first[:1], diag, 0.0))
    peaks.append(jnp.where(first[:1], 0.0, diag))
    peaks.append(jnp.zeros((2, LANES), F32))
    power = exponent(jnp.max(jnp.concatenate(peaks, axis=0), axis=1, keepdims=True))
    grow = 4096.0 * jnp.exp2(-power)
    powers = jnp.zeros((1, LANES), F32)
    for e in range(E_DEV):
        examples[e] = examples[e] * grow[e : e + 1]
        powers = jnp.where(lanes == me_ref[0] * E_DEV + e, power[e : e + 1], powers)
    out_ref[0:64, :] = jnp.where(first, examples[0], swap_halves(examples[1]))
    out_ref[64:128, :] = jnp.where(first, examples[2], swap_halves(examples[3]))
    parts = parts * (jnp.where(lanes < R, grow[4:5], grow[5:6]) * (1.0 / 32.0))
    other = swap_halves(parts)
    mixed = jnp.where(lane_iota(R) >= row_iota(R), parts, other)
    packed = jnp.where(first[:32], mixed[:32], swap_halves(mixed[32:]))
    diag = jnp.sum(jnp.where(on_diag, jnp.where(first, other, parts), 0.0), axis=0, keepdims=True)
    high = jnp.round(packed * 2.0) * 0.5
    diag_high = jnp.round(diag * 2.0) * 0.5
    diag = jnp.where(first[:1], diag_high, (diag - diag_high) * 1024.0)
    rows = row_iota(8)
    notes = jnp.zeros((8, LANES), F32)
    for i, line in enumerate([diag, power[4:5], power[5:6], powers, named.astype(F32)]):
        notes = jnp.where(rows == i, line, notes)
    out_ref[NOTES:HIGH, :] = notes
    out_ref[HIGH:LOW, :] = high
    out_ref[LOW:PACK, :] = (packed - high) * 1024.0


def project(x, g, pin, pout, me, ids, counts):
    hbm = pl.BlockSpec(memory_space=pl.ANY)
    smem = pl.BlockSpec(memory_space=pltpu.SMEM)
    return pl.pallas_call(
        project_kernel,
        out_shape=pltpu.VMEM((PACK, LANES), F32),
        in_specs=[hbm, hbm, hbm, hbm, smem, smem, smem],
        out_specs=pl.BlockSpec(memory_space=pltpu.VMEM),
        scratch_shapes=[
            pltpu.VMEM((ROWS, D), BF16),
            pltpu.VMEM((ROWS, D), BF16),
            pltpu.VMEM((R, D), BF16),
            pltpu.VMEM((R, D), BF16),
            pltpu.VMEM((LANES, ROWS), F32),
            pltpu.SemaphoreType.DMA((2 + 2 * CHUNKS,)),
        ],
        compiler_params=pltpu.CompilerParams(vmem_limit_bytes=60 * MIB),
        name="project",
    )(x, g, pin, pout, me, ids, counts)


def invert_pair(m):
    lanes = lane_iota(R)
    rows = row_iota(R)
    half = jnp.where(lanes < R, 0, R)
    local = lane_iota(1) % R
    for k in range(0, R, PANEL):
        columns = [jnp.take_along_axis(m, half + (k + i), axis=1) for i in range(PANEL)]
        lines = [m[k + i : k + i + 1] for i in range(PANEL)]
        inside = (local >= k) & (local < k + PANEL)
        steps = []
        for j in range(0, PANEL, 2):
            c0, c1 = columns[j], columns[j + 1]
            a, b = k + j, k + j + 1
            p00, p10 = c0[a : a + 1], c0[b : b + 1]
            p01, p11 = c1[a : a + 1], c1[b : b + 1]
            inv = 1.0 / (p00 * p11 - p01 * p10)
            s00, s01, s10, s11 = p11 * inv, p01 * inv, p10 * inv, p00 * inv
            is0, is1 = local == a, local == b
            r0 = jnp.where(is0, 1.0, jnp.where(is1, 0.0, lines[j]))
            r1 = jnp.where(is1, 1.0, jnp.where(is0, 0.0, lines[j + 1]))
            q0 = s00 * r0 - s01 * r1
            q1 = s11 * r1 - s10 * r0
            for i in range(PANEL):
                if i != j and i != j + 1:
                    u0, u1 = c0[k + i : k + i + 1], c1[k + i : k + i + 1]
                    lines[i] = jnp.where(is0 | is1, 0.0, lines[i]) - u0 * q0 - u1 * q1
            lines[j], lines[j + 1] = q0, q1
            for i in range(j + 2, PANEL):
                x0, x1 = columns[i][a : a + 1], columns[i][b : b + 1]
                y0 = s00 * x0 - s01 * x1
                y1 = s11 * x1 - s10 * x0
                column = columns[i] - c0 * y0 - c1 * y1
                columns[i] = jnp.where(rows == a, y0, jnp.where(rows == b, y1, column))
            steps = [(c, jnp.where(is0 | is1, 0.0, q)) for c, q in steps]
            steps += [(c0, q0), (c1, q1)]
        m = jnp.where(inside, 0.0, m)
        for c, q in steps:
            m = m - c * q
        for i in range(PANEL):
            m = jnp.where(rows == k + i, lines[i], m)
    return m


def block_diagonal(a):
    wide = jnp.concatenate([a, a], axis=1)
    tall = jnp.concatenate([wide, wide, wide, wide], axis=0)
    r = lax.broadcasted_iota(jnp.int32, (4 * R, 4 * R), 0) // R
    c = lax.broadcasted_iota(jnp.int32, (4 * R, 4 * R), 1) // R
    return jnp.where(r == c, tall, 0.0)


def precondition(t_ref, left, ah, al, lh, ll, u, tp_ref):
    for z in range(Z):
        th, tl = split(jnp.concatenate([t_ref[z, :R, :], t_ref[z, R : 2 * R, :]], axis=1))
        p = dot(left, th, NN)
        q = dot(left[: 2 * R], tl, NN)
        high, low = split(p[:R] + ((p[R : 2 * R] + q[:R]) + (p[2 * R :] + q[R:])))
        lh[z * R : (z + 1) * R, :] = high
        ll[z * R : (z + 1) * R, :] = low
    for c in range(2):
        rows = slice(c * 256, (c + 1) * 256)
        high = lh[rows, :]
        p = dot(high, ah, NN) + (dot(ll[rows, :], ah, NN) + dot(high, al, NN))
        for s in range(4):
            for t in range(2):
                pair = (c * 4 + s) * 2 + t
                u[pair * R : (pair + 1) * R, :] = p[s * R : (s + 1) * R, t * 128 : (t + 1) * 128]
    low_half = lane_iota(16) < R
    for i in range(0, R, 2):
        w0 = u[pl.ds(i, 16, stride=R), :]
        w1 = u[pl.ds(i + 1, 16, stride=R), :]
        cols = slice(i * R, (i + 2) * R)
        tp_ref[0:16, cols] = jnp.where(low_half, w0, swap_halves(w1)).astype(BF16)
        tp_ref[16:32, cols] = jnp.where(low_half, swap_halves(w0), w1).astype(BF16)


def solve_kernel(tokens, p0, p1, p2, p3, t_ref, tp_ref, left_ref, ah_ref, al_ref, lh, ll, u):
    total = (p0[...] + p2[...]) + (p1[...] + p3[...])
    first = lane_iota(R) < R
    row, col = row_iota(R), lane_iota(R) % R
    packed = total[8:]
    moved = swap_halves(packed)
    mixed = jnp.concatenate(
        [jnp.where(first[:32], packed, moved), jnp.where(first[:32], moved, packed)], axis=0
    )
    turned = jnp.concatenate([mixed, mixed], axis=0).T[:R]
    diag_g = total[0:1]
    moved = swap_halves(diag_g)
    diag_g = jnp.where(first[:1], diag_g, moved) + jnp.where(first[:1], moved, diag_g) * (1.0 / 1024.0)
    factor_a = jnp.where(col >= row, mixed, turned)
    factor_g = jnp.where(col < row, mixed, jnp.where(col > row, turned, diag_g))
    m = jnp.where(first, factor_a, factor_g) * (1.0 / tokens)
    on_diag = row == col
    diag = jnp.sum(jnp.where(on_diag, m, 0.0), axis=0, keepdims=True)
    trace_a = jnp.sum(jnp.where(first[:1], diag, 0.0), axis=1, keepdims=True)
    trace_g = jnp.sum(jnp.where(first[:1], 0.0, diag), axis=1, keepdims=True)
    damp = (DAMP / R) * jnp.where(first[:1], trace_a, trace_g) + 1e-06
    m = invert_pair(jnp.where(on_diag, m + damp, m))
    other = swap_halves(m)
    ah, al = split(block_diagonal(jnp.where(first, m, other)))
    ig = jnp.where(first, other, m)[:, :R]
    g0 = ig.astype(BF16)
    g1, g2 = split(ig - g0.astype(F32))
    left = jnp.concatenate([g0, g1, g2], axis=0)
    left_ref[...] = left
    ah_ref[...] = ah
    al_ref[...] = al
    precondition(t_ref, left, ah, al, lh, ll, u, tp_ref)


def solve(parts, wide, tokens):
    vmem = pl.BlockSpec(memory_space=pltpu.VMEM)
    return pl.pallas_call(
        lambda *refs: solve_kernel(float(tokens), *refs),
        out_shape=(
            jax.ShapeDtypeStruct((Z * E_DEV, D), BF16),
            jax.ShapeDtypeStruct((3 * R, R), BF16),
            jax.ShapeDtypeStruct((4 * R, 4 * R), BF16),
            jax.ShapeDtypeStruct((4 * R, 4 * R), BF16),
        ),
        in_specs=[vmem] * (Y + 1),
        out_specs=(vmem,) * 4,
        scratch_shapes=[
            pltpu.VMEM((Z * R, 256), BF16),
            pltpu.VMEM((Z * R, 256), BF16),
            pltpu.VMEM((2 * Z * R, LANES), F32),
        ],
        compiler_params=pltpu.CompilerParams(vmem_limit_bytes=32 * MIB),
        cost_estimate=pl.CostEstimate(flops=4 * 10**9, bytes_accessed=2 * MIB, transcendentals=0),
        name="solve",
    )(*parts, wide)


def score_kernel(
    scale, tp, left_ref, ah_ref, al_ref, wide, far, at_ref, q0, q1, out_ref, lh, ll, u, tq, names
):
    my_z, my_y, far_y = at_ref[0], at_ref[1], at_ref[2]
    precondition(far, left_ref[...], ah_ref[...], al_ref[...], lh, ll, u, tq)
    lanes = lane_iota(2 * Z)
    rows = row_iota(2 * Z)
    source = jnp.where(rows < Z, my_y, far_y)
    mine = (lanes // (Y * E_DEV) == rows % Z) & (lanes // E_DEV % Y == source)
    power = jnp.zeros((1, LANES), F32)
    listed = []
    for ref in (wide, far):
        for z in range(Z):
            power = power + ref[z, NOTES + 3 : NOTES + 4, :]
            listed.append(ref[z, NOTES + 4 : NOTES + 5, :])
    listed = jnp.concatenate(listed, axis=0).astype(BF16)
    names[...] = dot(listed, jnp.where(mine, 1.0, 0.0).astype(BF16), TN)
    named = names[pl.ds(pl.multiple_of(my_z * (Y * CAP), Y * CAP), Y * CAP), :]
    column = jnp.exp2(power) * scale

    examples = jnp.concatenate([tp[...], tq[...]], axis=0)
    s = jnp.concatenate([dot(q0[...], examples, NT), dot(q1[...], examples, NT)], axis=0)
    take = row_iota(64)
    y = jnp.where(take < 32, my_y, far_y)
    take = take % 32
    place = take % 16 // 2 * (Y * E_DEV) + y * E_DEV + take % 2 * 2 + take // 16
    onehot = jnp.where(place == lane_iota(64), 1.0, 0.0).astype(BF16)
    s0 = s.astype(BF16)
    s1, s2 = split(s - s0.astype(F32))
    s = dot(s0, onehot, NN) + (dot(s1, onehot, NN) + dot(s2, onehot, NN))
    blocks = (row_iota(R) // QB).astype(F32)
    for k in range(2):
        owner = my_y if k == 0 else my_y + 1 - my_y % 2 * 2
        id0, id1 = named[0:1], named[1:2]
        for y in range(1, Y):
            id0 = jnp.where(owner == y, named[2 * y : 2 * y + 1], id0)
            id1 = jnp.where(owner == y, named[2 * y + 1 : 2 * y + 2], id1)
        live = (blocks == id0) | (blocks == id1)
        out_ref[owner % 2] = jnp.where(live, s[k * R : (k + 1) * R] * column, 0.0)


def score(solved, wide, far, at, queries, scale):
    vmem = pl.BlockSpec(memory_space=pltpu.VMEM)
    smem = pl.BlockSpec(memory_space=pltpu.SMEM)
    return pl.pallas_call(
        lambda *refs: score_kernel(scale, *refs),
        out_shape=jax.ShapeDtypeStruct((2, R, LANES), F32),
        in_specs=[vmem] * 6 + [smem] + [vmem] * 2,
        out_specs=vmem,
        scratch_shapes=[
            pltpu.VMEM((Z * R, 256), BF16),
            pltpu.VMEM((Z * R, 256), BF16),
            pltpu.VMEM((2 * Z * R, LANES), F32),
            pltpu.VMEM((Z * E_DEV, D), BF16),
            pltpu.VMEM((LANES, LANES), F32),
        ],
        compiler_params=pltpu.CompilerParams(vmem_limit_bytes=32 * MIB),
        cost_estimate=pl.CostEstimate(flops=10**9, bytes_accessed=3 * MIB, transcendentals=0),
        name="score",
    )(*solved, wide, far, at, *queries)


def body(x_act, g_out, proj_in, proj_out, queries, cand_ids, cand_counts):
    n_layers = lax.axis_size("block")
    my_z = lax.axis_index("z").astype(jnp.int32)
    my_y = lax.axis_index(("yh", "yl")).astype(jnp.int32)
    me = my_z * Y + my_y
    far_y = (my_y + 3 + my_y % 2 * 2) % Y
    near = lax.ppermute(queries[0], "yl", [(0, 1), (1, 0)])
    packet = project(
        x_act[0],
        g_out[0],
        proj_in[0].T,
        proj_out[0].T,
        jnp.reshape(me, (1,)),
        cand_ids[0].T,
        cand_counts,
    )
    packet = jnp.broadcast_to(packet.astype(F16)[None], (Z, PACK, LANES))
    got = lax.all_to_all(packet, "z", 0, 0, tiled=True)

    r = jnp.arange(LOW - NOTES)[:, None] - (HIGH - NOTES)
    lane = jnp.arange(LANES)[None, :]
    upper = (lane % R >= r + R // 2 * (lane // R)) & (r >= 0)
    power = jnp.where(
        upper[None],
        got[:, NOTES + 1 : NOTES + 2].astype(F32),
        got[:, NOTES + 2 : NOTES + 3].astype(F32),
    )
    low = jnp.pad(got[:, LOW:].astype(F32), ((0, 0), (HIGH - NOTES, 0), (0, 0)))
    both = got[:, NOTES:LOW].astype(F32) + low * (1.0 / 1024.0)
    sums = jnp.sum(both * (jnp.exp2(power) * (1.0 / 128.0)), axis=0)
    parts = [sums] + [
        lax.ppermute(sums, ("yh", "yl"), [(y, (y + k) % Y) for y in range(Y)]) for k in range(1, Y)
    ]
    sums, got = lax.optimization_barrier((sums, got))
    own = got[:, :HIGH]
    far = lax.ppermute(own, ("yh", "yl"), [(0, 3), (3, 0), (1, 2), (2, 1)])

    scale = 1.0 / float(R * R * n_layers) ** 0.5 / 4096.0
    wide = own.astype(F32)
    solved = solve(parts, wide, ROWS * Z * Y)
    at = jnp.stack([my_z, my_y, far_y])
    scores = score(solved, wide, far.astype(F32), at, [queries[0], near], scale)
    scores = scores.reshape(2 * n_layers, R // n_layers, LANES)
    return jnp.sum(lax.all_to_all(scores, ("yl", "block"), 0, 0, tiled=True), axis=0)


def solution(mesh):
    axes = ("z", "yh", "yl", "block")
    split_mesh = Mesh(mesh.devices.reshape(Z, 2, 2, -1), axes)
    shard = axes[:3]
    return jax.shard_map(
        body,
        mesh=split_mesh,
        in_specs=(
            P("block", shard, None),
            P("block", shard, None),
            P("block", None, None),
            P("block", None, None),
            P("block", shard, None),
            P(shard, None, None),
            P(shard, None),
        ),
        out_specs=P(axes, None),
        check_vma=False,
    )
```

```python
import jax
import jax.numpy as jnp
from jax import lax
from jax.experimental import pallas as pl
from jax.experimental.pallas import tpu as pltpu
from jax.sharding import Mesh
from jax.sharding import PartitionSpec as P

E_DEV = 4
SEQ = 128
QB = 4
CAP = 2
Z = 8
Y = 4
R = 64
LANES = 128
ROWS = E_DEV * SEQ
D = 4096
F16 = jnp.float16
F32 = jnp.float32
BF16 = jnp.bfloat16
DAMP = 0.1
NT = (((1,), (1,)), ((), ()))
NN = (((1,), (0,)), ((), ()))
TN = (((0,), (0,)), ((), ()))
CHUNKS = 8
WIDTH = D // CHUNKS
PANEL = 8
MIB = 1024 * 1024

NOTES = 128
HIGH = 136
LOW = 168
PACK = 200


def dot(a, b, dims):
    return lax.dot_general(a, b, dims, preferred_element_type=F32)


def lane_iota(rows):
    return lax.broadcasted_iota(jnp.int32, (rows, LANES), 1)


def row_iota(rows):
    return lax.broadcasted_iota(jnp.int32, (rows, LANES), 0)


def swap_halves(x):
    return pltpu.roll(x, R, 1)


def exponent(m):
    return jnp.clip(jnp.floor(jnp.log2(jnp.maximum(m, 1e-30))), -96.0, 126.0)


def split(x):
    high = x.astype(BF16)
    return high, (x - high.astype(F32)).astype(BF16)


def project_kernel(
    x_hbm, g_hbm, pin_hbm, pout_hbm, me_ref, ids_ref, counts_ref, out_ref, x, g, pin, pout, acc, sem
):
    copies = []

    def fetch(src, dst):
        copy = pltpu.make_async_copy(src, dst, sem.at[len(copies)])
        copy.start()
        copies.append(copy)
        return copy

    pin_copy = fetch(pin_hbm, pin)
    x_copies, g_copies = [], []
    for c in range(CHUNKS):
        cols = slice(c * WIDTH, (c + 1) * WIDTH)
        x_copies.append(fetch(x_hbm.at[:, cols], x.at[:, cols]))
        if c == 0:
            pout_copy = fetch(pout_hbm, pout)
        g_copies.append(fetch(g_hbm.at[:, cols], g.at[:, cols]))

    lanes = lane_iota(1)
    named = jnp.zeros((1, LANES), jnp.int32)
    for owner in range(Z * Y):
        for slot in range(CAP):
            block = jnp.where(slot < counts_ref[0, owner], ids_ref[slot, owner], 99)
            named = jnp.where(lanes == owner * CAP + slot, block, named)

    pin_copy.wait()
    for c in range(CHUNKS):
        cols = slice(c * WIDTH, (c + 1) * WIDTH)
        x_copies[c].wait()
        xp = dot(pin[:, cols], x[:, cols], NT)
        if c == 0:
            pout_copy.wait()
        g_copies[c].wait()
        gp = dot(pout[:, cols], g[:, cols], NT)
        if c == 0:
            acc[:R] = xp
            acc[R:] = gp
        else:
            acc[:R] += xp
            acc[R:] += gp

    first = lane_iota(R) < R
    both = acc[...].astype(BF16)
    on_diag = row_iota(R) == lane_iota(R) % R
    total = jnp.zeros((LANES, LANES), F32)
    examples, peaks = [], []
    for e in range(E_DEV):
        cols = both[:, e * SEQ : (e + 1) * SEQ]
        gram = dot(cols, cols, NT)
        total = total + gram
        example = jnp.where(first, gram[R:], 0.0) * (1.0 / SEQ)
        examples.append(example)
        peaks.append(jnp.max(jnp.abs(example), axis=0, keepdims=True))
    parts = jnp.where(first, total[:R], total[R:])
    diag = jnp.max(jnp.where(on_diag, parts, 0.0), axis=0, keepdims=True)
    peaks.append(jnp.where(first[:1], diag, 0.0))
    peaks.append(jnp.where(first[:1], 0.0, diag))
    peaks.append(jnp.zeros((2, LANES), F32))
    power = exponent(jnp.max(jnp.concatenate(peaks, axis=0), axis=1, keepdims=True))
    grow = 4096.0 * jnp.exp2(-power)
    powers = jnp.zeros((1, LANES), F32)
    for e in range(E_DEV):
        examples[e] = examples[e] * grow[e : e + 1]
        powers = jnp.where(lanes == me_ref[0] * E_DEV + e, power[e : e + 1], powers)
    out_ref[0:64, :] = jnp.where(first, examples[0], swap_halves(examples[1]))
    out_ref[64:128, :] = jnp.where(first, examples[2], swap_halves(examples[3]))
    parts = parts * (jnp.where(lanes < R, grow[4:5], grow[5:6]) * (1.0 / 32.0))
    other = swap_halves(parts)
    mixed = jnp.where(lane_iota(R) >= row_iota(R), parts, other)
    packed = jnp.where(first[:32], mixed[:32], swap_halves(mixed[32:]))
    diag = jnp.sum(jnp.where(on_diag, jnp.where(first, other, parts), 0.0), axis=0, keepdims=True)
    high = jnp.round(packed * 2.0) * 0.5
    diag_high = jnp.round(diag * 2.0) * 0.5
    diag = jnp.where(first[:1], diag_high, (diag - diag_high) * 1024.0)
    rows = row_iota(8)
    notes = jnp.zeros((8, LANES), F32)
    for i, line in enumerate([diag, power[4:5], power[5:6], powers, named.astype(F32)]):
        notes = jnp.where(rows == i, line, notes)
    out_ref[NOTES:HIGH, :] = notes
    out_ref[HIGH:LOW, :] = high
    out_ref[LOW:PACK, :] = (packed - high) * 1024.0


def project(x, g, pin, pout, me, ids, counts):
    hbm = pl.BlockSpec(memory_space=pl.ANY)
    smem = pl.BlockSpec(memory_space=pltpu.SMEM)
    return pl.pallas_call(
        project_kernel,
        out_shape=pltpu.VMEM((PACK, LANES), F32),
        in_specs=[hbm, hbm, hbm, hbm, smem, smem, smem],
        out_specs=pl.BlockSpec(memory_space=pltpu.VMEM),
        scratch_shapes=[
            pltpu.VMEM((ROWS, D), BF16),
            pltpu.VMEM((ROWS, D), BF16),
            pltpu.VMEM((R, D), BF16),
            pltpu.VMEM((R, D), BF16),
            pltpu.VMEM((LANES, ROWS), F32),
            pltpu.SemaphoreType.DMA((2 + 2 * CHUNKS,)),
        ],
        compiler_params=pltpu.CompilerParams(vmem_limit_bytes=60 * MIB),
        name="project",
    )(x, g, pin, pout, me, ids, counts)


def invert_pair(m):
    lanes = lane_iota(R)
    rows = row_iota(R)
    half = jnp.where(lanes < R, 0, R)
    local = lane_iota(1) % R
    for k in range(0, R, PANEL):
        columns = [jnp.take_along_axis(m, half + (k + i), axis=1) for i in range(PANEL)]
        lines = [m[k + i : k + i + 1] for i in range(PANEL)]
        inside = (local >= k) & (local < k + PANEL)
        steps = []
        for j in range(0, PANEL, 2):
            c0, c1 = columns[j], columns[j + 1]
            a, b = k + j, k + j + 1
            p00, p10 = c0[a : a + 1], c0[b : b + 1]
            p01, p11 = c1[a : a + 1], c1[b : b + 1]
            inv = 1.0 / (p00 * p11 - p01 * p10)
            s00, s01, s10, s11 = p11 * inv, p01 * inv, p10 * inv, p00 * inv
            is0, is1 = local == a, local == b
            r0 = jnp.where(is0, 1.0, jnp.where(is1, 0.0, lines[j]))
            r1 = jnp.where(is1, 1.0, jnp.where(is0, 0.0, lines[j + 1]))
            q0 = s00 * r0 - s01 * r1
            q1 = s11 * r1 - s10 * r0
            for i in range(PANEL):
                if i != j and i != j + 1:
                    u0, u1 = c0[k + i : k + i + 1], c1[k + i : k + i + 1]
                    lines[i] = jnp.where(is0 | is1, 0.0, lines[i]) - u0 * q0 - u1 * q1
            lines[j], lines[j + 1] = q0, q1
            for i in range(j + 2, PANEL):
                x0, x1 = columns[i][a : a + 1], columns[i][b : b + 1]
                y0 = s00 * x0 - s01 * x1
                y1 = s11 * x1 - s10 * x0
                column = columns[i] - c0 * y0 - c1 * y1
                columns[i] = jnp.where(rows == a, y0, jnp.where(rows == b, y1, column))
            steps = [(c, jnp.where(is0 | is1, 0.0, q)) for c, q in steps]
            steps += [(c0, q0), (c1, q1)]
        m = jnp.where(inside, 0.0, m)
        for c, q in steps:
            m = m - c * q
        for i in range(PANEL):
            m = jnp.where(rows == k + i, lines[i], m)
    return m


def block_diagonal(a):
    wide = jnp.concatenate([a, a], axis=1)
    tall = jnp.concatenate([wide, wide, wide, wide], axis=0)
    r = lax.broadcasted_iota(jnp.int32, (4 * R, 4 * R), 0) // R
    c = lax.broadcasted_iota(jnp.int32, (4 * R, 4 * R), 1) // R
    return jnp.where(r == c, tall, 0.0)


def precondition(t_ref, left, ah, al, lh, ll, u, tp_ref):
    for z in range(Z):
        th, tl = split(jnp.concatenate([t_ref[z, :R, :], t_ref[z, R : 2 * R, :]], axis=1))
        p = dot(left, th, NN)
        q = dot(left[: 2 * R], tl, NN)
        high, low = split(p[:R] + ((p[R : 2 * R] + q[:R]) + (p[2 * R :] + q[R:])))
        lh[z * R : (z + 1) * R, :] = high
        ll[z * R : (z + 1) * R, :] = low
    for c in range(2):
        rows = slice(c * 256, (c + 1) * 256)
        high = lh[rows, :]
        p = dot(high, ah, NN) + (dot(ll[rows, :], ah, NN) + dot(high, al, NN))
        for s in range(4):
            for t in range(2):
                pair = (c * 4 + s) * 2 + t
                u[pair * R : (pair + 1) * R, :] = p[s * R : (s + 1) * R, t * 128 : (t + 1) * 128]
    low_half = lane_iota(16) < R
    for i in range(0, R, 2):
        w0 = u[pl.ds(i, 16, stride=R), :]
        w1 = u[pl.ds(i + 1, 16, stride=R), :]
        cols = slice(i * R, (i + 2) * R)
        tp_ref[0:16, cols] = jnp.where(low_half, w0, swap_halves(w1)).astype(BF16)
        tp_ref[16:32, cols] = jnp.where(low_half, swap_halves(w0), w1).astype(BF16)


def solve_kernel(tokens, p0, p1, p2, p3, t_ref, tp_ref, left_ref, ah_ref, al_ref, power_ref, lh, ll, u):
    total = (p0[...] + p2[...]) + (p1[...] + p3[...])
    first = lane_iota(R) < R
    row, col = row_iota(R), lane_iota(R) % R
    packed = total[8:]
    moved = swap_halves(packed)
    mixed = jnp.concatenate(
        [jnp.where(first[:32], packed, moved), jnp.where(first[:32], moved, packed)], axis=0
    )
    turned = jnp.concatenate([mixed, mixed], axis=0).T[:R]
    diag_g = total[0:1]
    moved = swap_halves(diag_g)
    diag_g = jnp.where(first[:1], diag_g, moved) + jnp.where(first[:1], moved, diag_g) * (1.0 / 1024.0)
    factor_a = jnp.where(col >= row, mixed, turned)
    factor_g = jnp.where(col < row, mixed, jnp.where(col > row, turned, diag_g))
    m = jnp.where(first, factor_a, factor_g) * (1.0 / tokens)
    on_diag = row == col
    diag = jnp.sum(jnp.where(on_diag, m, 0.0), axis=0, keepdims=True)
    trace_a = jnp.sum(jnp.where(first[:1], diag, 0.0), axis=1, keepdims=True)
    trace_g = jnp.sum(jnp.where(first[:1], 0.0, diag), axis=1, keepdims=True)
    damp = (DAMP / R) * jnp.where(first[:1], trace_a, trace_g) + 1e-06
    power_a = exponent(trace_a + R * damp[:, :1])
    power_g = exponent(trace_g + R * damp[:, R : R + 1])
    power_ref[...] = jnp.broadcast_to(power_a + power_g, (8, LANES))
    shrink = jnp.exp2(-jnp.where(first[:1], power_a, power_g))
    m = invert_pair(jnp.where(on_diag, m + damp, m) * shrink)
    other = swap_halves(m)
    ah, al = split(block_diagonal(jnp.where(first, m, other)))
    ig = jnp.where(first, other, m)[:, :R]
    g0 = ig.astype(BF16)
    g1, g2 = split(ig - g0.astype(F32))
    left = jnp.concatenate([g0, g1, g2], axis=0)
    left_ref[...] = left
    ah_ref[...] = ah
    al_ref[...] = al
    precondition(t_ref, left, ah, al, lh, ll, u, tp_ref)


def solve(parts, wide, tokens):
    vmem = pl.BlockSpec(memory_space=pltpu.VMEM)
    return pl.pallas_call(
        lambda *refs: solve_kernel(float(tokens), *refs),
        out_shape=(
            jax.ShapeDtypeStruct((Z * E_DEV, D), BF16),
            jax.ShapeDtypeStruct((3 * R, R), BF16),
            jax.ShapeDtypeStruct((4 * R, 4 * R), BF16),
            jax.ShapeDtypeStruct((4 * R, 4 * R), BF16),
            jax.ShapeDtypeStruct((8, LANES), F32),
        ),
        in_specs=[vmem] * (Y + 1),
        out_specs=(vmem,) * 5,
        scratch_shapes=[
            pltpu.VMEM((Z * R, 256), BF16),
            pltpu.VMEM((Z * R, 256), BF16),
            pltpu.VMEM((2 * Z * R, LANES), F32),
        ],
        compiler_params=pltpu.CompilerParams(vmem_limit_bytes=32 * MIB),
        cost_estimate=pl.CostEstimate(flops=4 * 10**9, bytes_accessed=2 * MIB, transcendentals=0),
        name="solve",
    )(*parts, wide)


def score_kernel(
    scale, tp, left_ref, ah_ref, al_ref, power_ref, wide, far, at_ref, q0, q1, out_ref, lh, ll, u, tq, names
):
    my_z, my_y, far_y = at_ref[0], at_ref[1], at_ref[2]
    precondition(far, left_ref[...], ah_ref[...], al_ref[...], lh, ll, u, tq)
    lanes = lane_iota(2 * Z)
    rows = row_iota(2 * Z)
    source = jnp.where(rows < Z, my_y, far_y)
    mine = (lanes // (Y * E_DEV) == rows % Z) & (lanes // E_DEV % Y == source)
    power = jnp.zeros((1, LANES), F32)
    listed = []
    for ref in (wide, far):
        for z in range(Z):
            power = power + ref[z, NOTES + 3 : NOTES + 4, :]
            listed.append(ref[z, NOTES + 4 : NOTES + 5, :])
    listed = jnp.concatenate(listed, axis=0).astype(BF16)
    names[...] = dot(listed, jnp.where(mine, 1.0, 0.0).astype(BF16), TN)
    named = names[pl.ds(pl.multiple_of(my_z * (Y * CAP), Y * CAP), Y * CAP), :]
    column = jnp.exp2(power - power_ref[0:1, :]) * scale

    examples = jnp.concatenate([tp[...], tq[...]], axis=0)
    s = jnp.concatenate([dot(q0[...], examples, NT), dot(q1[...], examples, NT)], axis=0)
    take = row_iota(64)
    y = jnp.where(take < 32, my_y, far_y)
    take = take % 32
    place = take % 16 // 2 * (Y * E_DEV) + y * E_DEV + take % 2 * 2 + take // 16
    onehot = jnp.where(place == lane_iota(64), 1.0, 0.0).astype(BF16)
    s0 = s.astype(BF16)
    s1, s2 = split(s - s0.astype(F32))
    s = dot(s0, onehot, NN) + (dot(s1, onehot, NN) + dot(s2, onehot, NN))
    blocks = (row_iota(R) // QB).astype(F32)
    for k in range(2):
        owner = my_y if k == 0 else my_y + 1 - my_y % 2 * 2
        id0, id1 = named[0:1], named[1:2]
        for y in range(1, Y):
            id0 = jnp.where(owner == y, named[2 * y : 2 * y + 1], id0)
            id1 = jnp.where(owner == y, named[2 * y + 1 : 2 * y + 2], id1)
        live = (blocks == id0) | (blocks == id1)
        out_ref[owner % 2] = jnp.where(live, s[k * R : (k + 1) * R] * column, 0.0)


def score(solved, wide, far, at, queries, scale):
    vmem = pl.BlockSpec(memory_space=pltpu.VMEM)
    smem = pl.BlockSpec(memory_space=pltpu.SMEM)
    return pl.pallas_call(
        lambda *refs: score_kernel(scale, *refs),
        out_shape=jax.ShapeDtypeStruct((2, R, LANES), F32),
        in_specs=[vmem] * 7 + [smem] + [vmem] * 2,
        out_specs=vmem,
        scratch_shapes=[
            pltpu.VMEM((Z * R, 256), BF16),
            pltpu.VMEM((Z * R, 256), BF16),
            pltpu.VMEM((2 * Z * R, LANES), F32),
            pltpu.VMEM((Z * E_DEV, D), BF16),
            pltpu.VMEM((LANES, LANES), F32),
        ],
        compiler_params=pltpu.CompilerParams(vmem_limit_bytes=32 * MIB),
        cost_estimate=pl.CostEstimate(flops=10**9, bytes_accessed=3 * MIB, transcendentals=0),
        name="score",
    )(*solved, wide, far, at, *queries)


def body(x_act, g_out, proj_in, proj_out, queries, cand_ids, cand_counts):
    n_layers = lax.axis_size("block")
    my_z = lax.axis_index("z").astype(jnp.int32)
    my_y = lax.axis_index(("yh", "yl")).astype(jnp.int32)
    me = my_z * Y + my_y
    far_y = (my_y + 3 + my_y % 2 * 2) % Y
    near = lax.ppermute(queries[0], "yl", [(0, 1), (1, 0)])
    packet = project(
        x_act[0],
        g_out[0],
        proj_in[0].T,
        proj_out[0].T,
        jnp.reshape(me, (1,)),
        cand_ids[0].T,
        cand_counts,
    )
    packet = jnp.broadcast_to(packet.astype(F16)[None], (Z, PACK, LANES))
    got = lax.all_to_all(packet, "z", 0, 0, tiled=True)

    r = jnp.arange(LOW - NOTES)[:, None] - (HIGH - NOTES)
    lane = jnp.arange(LANES)[None, :]
    upper = (lane % R >= r + R // 2 * (lane // R)) & (r >= 0)
    power = jnp.where(
        upper[None],
        got[:, NOTES + 1 : NOTES + 2].astype(F32),
        got[:, NOTES + 2 : NOTES + 3].astype(F32),
    )
    low = jnp.pad(got[:, LOW:].astype(F32), ((0, 0), (HIGH - NOTES, 0), (0, 0)))
    both = got[:, NOTES:LOW].astype(F32) + low * (1.0 / 1024.0)
    sums = jnp.sum(both * (jnp.exp2(power) * (1.0 / 128.0)), axis=0)
    parts = [sums] + [
        lax.ppermute(sums, ("yh", "yl"), [(y, (y + k) % Y) for y in range(Y)]) for k in range(1, Y)
    ]
    sums, got = lax.optimization_barrier((sums, got))
    own = got[:, :HIGH]
    far = lax.ppermute(own, ("yh", "yl"), [(0, 3), (3, 0), (1, 2), (2, 1)])

    scale = 1.0 / float(R * R * n_layers) ** 0.5 / 4096.0
    wide = own.astype(F32)
    solved = solve(parts, wide, ROWS * Z * Y)
    at = jnp.stack([my_z, my_y, far_y])
    scores = score(solved, wide, far.astype(F32), at, [queries[0], near], scale)
    scores = scores.reshape(2 * n_layers, R // n_layers, LANES)
    return jnp.sum(lax.all_to_all(scores, ("yl", "block"), 0, 0, tiled=True), axis=0)


def solution(mesh):
    axes = ("z", "yh", "yl", "block")
    split_mesh = Mesh(mesh.devices.reshape(Z, 2, 2, -1), axes)
    shard = axes[:3]
    return jax.shard_map(
        body,
        mesh=split_mesh,
        in_specs=(
            P("block", shard, None),
            P("block", shard, None),
            P("block", None, None),
            P("block", None, None),
            P("block", shard, None),
            P(shard, None, None),
            P(shard, None),
        ),
        out_specs=P(axes, None),
        check_vma=False,
    )
```

```python
import jax
import jax.numpy as jnp
from jax import lax
from jax.experimental import pallas as pl
from jax.experimental.pallas import tpu as pltpu
from jax.sharding import Mesh
from jax.sharding import PartitionSpec as P

E_DEV = 4
SEQ = 128
QB = 4
CAP = 2
Z = 8
Y = 4
R = 64
LANES = 128
ROWS = E_DEV * SEQ
D = 4096
F16 = jnp.float16
F32 = jnp.float32
BF16 = jnp.bfloat16
DAMP = 0.1
NT = (((1,), (1,)), ((), ()))
NN = (((1,), (0,)), ((), ()))
TN = (((0,), (0,)), ((), ()))
EDGES = [0, 512, 1024, 1536, 2048, 2560, 3072, 3584, 3840, D]
CHUNKS = len(EDGES) - 1
PANEL = 8
MIB = 1024 * 1024

NOTES = 128
HIGH = 136
LOW = 168
PACK = 200


def dot(a, b, dims):
    return lax.dot_general(a, b, dims, preferred_element_type=F32)


def lane_iota(rows):
    return lax.broadcasted_iota(jnp.int32, (rows, LANES), 1)


def row_iota(rows):
    return lax.broadcasted_iota(jnp.int32, (rows, LANES), 0)


def swap_halves(x):
    return pltpu.roll(x, R, 1)


def exponent(m):
    return jnp.clip(jnp.floor(jnp.log2(jnp.maximum(m, 1e-30))), -96.0, 126.0)


def split(x):
    high = x.astype(BF16)
    return high, (x - high.astype(F32)).astype(BF16)


def project_kernel(
    x_hbm, g_hbm, pin_hbm, pout_hbm, me_ref, ids_ref, counts_ref, out_ref, x, g, pin, pout, acc, sem
):
    copies = []

    def fetch(src, dst):
        copy = pltpu.make_async_copy(src, dst, sem.at[len(copies)])
        copy.start()
        copies.append(copy)
        return copy

    pin_copy = fetch(pin_hbm, pin)
    x_copies, g_copies = [], []
    for c in range(CHUNKS):
        cols = slice(EDGES[c], EDGES[c + 1])
        x_copies.append(fetch(x_hbm.at[:, cols], x.at[:, cols]))
        if c == 0:
            pout_copy = fetch(pout_hbm, pout)
        g_copies.append(fetch(g_hbm.at[:, cols], g.at[:, cols]))

    lanes = lane_iota(1)
    named = jnp.zeros((1, LANES), jnp.int32)
    for owner in range(Z * Y):
        for slot in range(CAP):
            block = jnp.where(slot < counts_ref[0, owner], ids_ref[slot, owner], 99)
            named = jnp.where(lanes == owner * CAP + slot, block, named)

    pin_copy.wait()
    for c in range(CHUNKS):
        cols = slice(EDGES[c], EDGES[c + 1])
        x_copies[c].wait()
        xp = dot(pin[:, cols], x[:, cols], NT)
        if c == 0:
            pout_copy.wait()
        g_copies[c].wait()
        gp = dot(pout[:, cols], g[:, cols], NT)
        if c == 0:
            acc[:R] = xp
            acc[R:] = gp
        else:
            acc[:R] += xp
            acc[R:] += gp

    first = lane_iota(R) < R
    both = acc[...].astype(BF16)
    on_diag = row_iota(R) == lane_iota(R) % R
    total = jnp.zeros((LANES, LANES), F32)
    examples, peaks = [], []
    for e in range(E_DEV):
        cols = both[:, e * SEQ : (e + 1) * SEQ]
        gram = dot(cols, cols, NT)
        total = total + gram
        example = jnp.where(first, gram[R:], 0.0) * (1.0 / SEQ)
        examples.append(example)
        peaks.append(jnp.max(jnp.abs(example), axis=0, keepdims=True))
    parts = jnp.where(first, total[:R], total[R:])
    diag = jnp.max(jnp.where(on_diag, parts, 0.0), axis=0, keepdims=True)
    peaks.append(jnp.where(first[:1], diag, 0.0))
    peaks.append(jnp.where(first[:1], 0.0, diag))
    peaks.append(jnp.zeros((2, LANES), F32))
    power = exponent(jnp.max(jnp.concatenate(peaks, axis=0), axis=1, keepdims=True))
    grow = 4096.0 * jnp.exp2(-power)
    powers = jnp.zeros((1, LANES), F32)
    for e in range(E_DEV):
        examples[e] = examples[e] * grow[e : e + 1]
        powers = jnp.where(lanes == me_ref[0] * E_DEV + e, power[e : e + 1], powers)
    out_ref[0:64, :] = jnp.where(first, examples[0], swap_halves(examples[1]))
    out_ref[64:128, :] = jnp.where(first, examples[2], swap_halves(examples[3]))
    parts = parts * (jnp.where(lanes < R, grow[4:5], grow[5:6]) * (1.0 / 32.0))
    other = swap_halves(parts)
    mixed = jnp.where(lane_iota(R) >= row_iota(R), parts, other)
    packed = jnp.where(first[:32], mixed[:32], swap_halves(mixed[32:]))
    diag = jnp.sum(jnp.where(on_diag, jnp.where(first, other, parts), 0.0), axis=0, keepdims=True)
    high = jnp.round(packed * 2.0) * 0.5
    diag_high = jnp.round(diag * 2.0) * 0.5
    diag = jnp.where(first[:1], diag_high, (diag - diag_high) * 1024.0)
    rows = row_iota(8)
    notes = jnp.zeros((8, LANES), F32)
    for i, line in enumerate([diag, power[4:5], power[5:6], powers, named.astype(F32)]):
        notes = jnp.where(rows == i, line, notes)
    out_ref[NOTES:HIGH, :] = notes
    out_ref[HIGH:LOW, :] = high
    out_ref[LOW:PACK, :] = (packed - high) * 1024.0


def project(x, g, pin, pout, me, ids, counts):
    hbm = pl.BlockSpec(memory_space=pl.ANY)
    smem = pl.BlockSpec(memory_space=pltpu.SMEM)
    return pl.pallas_call(
        project_kernel,
        out_shape=pltpu.VMEM((PACK, LANES), F32),
        in_specs=[hbm, hbm, hbm, hbm, smem, smem, smem],
        out_specs=pl.BlockSpec(memory_space=pltpu.VMEM),
        scratch_shapes=[
            pltpu.VMEM((ROWS, D), BF16),
            pltpu.VMEM((ROWS, D), BF16),
            pltpu.VMEM((R, D), BF16),
            pltpu.VMEM((R, D), BF16),
            pltpu.VMEM((LANES, ROWS), F32),
            pltpu.SemaphoreType.DMA((2 + 2 * CHUNKS,)),
        ],
        compiler_params=pltpu.CompilerParams(vmem_limit_bytes=60 * MIB),
        name="project",
    )(x, g, pin, pout, me, ids, counts)


def invert_pair(m):
    lanes = lane_iota(R)
    rows = row_iota(R)
    half = jnp.where(lanes < R, 0, R)
    local = lane_iota(1) % R
    for k in range(0, R, PANEL):
        columns = [jnp.take_along_axis(m, half + (k + i), axis=1) for i in range(PANEL)]
        lines = [m[k + i : k + i + 1] for i in range(PANEL)]
        inside = (local >= k) & (local < k + PANEL)
        steps = []
        for j in range(0, PANEL, 2):
            c0, c1 = columns[j], columns[j + 1]
            a, b = k + j, k + j + 1
            p00, p10 = c0[a : a + 1], c0[b : b + 1]
            p01, p11 = c1[a : a + 1], c1[b : b + 1]
            inv = 1.0 / (p00 * p11 - p01 * p10)
            s00, s01, s10, s11 = p11 * inv, p01 * inv, p10 * inv, p00 * inv
            is0, is1 = local == a, local == b
            r0 = jnp.where(is0, 1.0, jnp.where(is1, 0.0, lines[j]))
            r1 = jnp.where(is1, 1.0, jnp.where(is0, 0.0, lines[j + 1]))
            q0 = s00 * r0 - s01 * r1
            q1 = s11 * r1 - s10 * r0
            for i in range(PANEL):
                if i != j and i != j + 1:
                    u0, u1 = c0[k + i : k + i + 1], c1[k + i : k + i + 1]
                    lines[i] = jnp.where(is0 | is1, 0.0, lines[i]) - u0 * q0 - u1 * q1
            lines[j], lines[j + 1] = q0, q1
            for i in range(j + 2, PANEL):
                x0, x1 = columns[i][a : a + 1], columns[i][b : b + 1]
                y0 = s00 * x0 - s01 * x1
                y1 = s11 * x1 - s10 * x0
                column = columns[i] - c0 * y0 - c1 * y1
                columns[i] = jnp.where(rows == a, y0, jnp.where(rows == b, y1, column))
            steps = [(c, jnp.where(is0 | is1, 0.0, q)) for c, q in steps]
            steps += [(c0, q0), (c1, q1)]
        m = jnp.where(inside, 0.0, m)
        for c, q in steps:
            m = m - c * q
        for i in range(PANEL):
            m = jnp.where(rows == k + i, lines[i], m)
    return m


def block_diagonal(a):
    wide = jnp.concatenate([a, a], axis=1)
    tall = jnp.concatenate([wide, wide, wide, wide], axis=0)
    r = lax.broadcasted_iota(jnp.int32, (4 * R, 4 * R), 0) // R
    c = lax.broadcasted_iota(jnp.int32, (4 * R, 4 * R), 1) // R
    return jnp.where(r == c, tall, 0.0)


def precondition(t_ref, left, ah, al, lh, ll, u, tp_ref):
    for z in range(Z):
        th, tl = split(jnp.concatenate([t_ref[z, :R, :], t_ref[z, R : 2 * R, :]], axis=1))
        p = dot(left, th, NN)
        q = dot(left[: 2 * R], tl, NN)
        high, low = split(p[:R] + ((p[R : 2 * R] + q[:R]) + (p[2 * R :] + q[R:])))
        lh[z * R : (z + 1) * R, :] = high
        ll[z * R : (z + 1) * R, :] = low
    for c in range(2):
        rows = slice(c * 256, (c + 1) * 256)
        high = lh[rows, :]
        p = dot(high, ah, NN) + (dot(ll[rows, :], ah, NN) + dot(high, al, NN))
        for s in range(4):
            for t in range(2):
                pair = (c * 4 + s) * 2 + t
                u[pair * R : (pair + 1) * R, :] = p[s * R : (s + 1) * R, t * 128 : (t + 1) * 128]
    low_half = lane_iota(16) < R
    for i in range(0, R, 2):
        w0 = u[pl.ds(i, 16, stride=R), :]
        w1 = u[pl.ds(i + 1, 16, stride=R), :]
        cols = slice(i * R, (i + 2) * R)
        tp_ref[0:16, cols] = jnp.where(low_half, w0, swap_halves(w1)).astype(BF16)
        tp_ref[16:32, cols] = jnp.where(low_half, swap_halves(w0), w1).astype(BF16)


def solve_kernel(tokens, p0, p1, p2, p3, t_ref, tp_ref, left_ref, ah_ref, al_ref, power_ref, lh, ll, u):
    total = (p0[...] + p2[...]) + (p1[...] + p3[...])
    first = lane_iota(R) < R
    row, col = row_iota(R), lane_iota(R) % R
    packed = total[8:]
    moved = swap_halves(packed)
    mixed = jnp.concatenate(
        [jnp.where(first[:32], packed, moved), jnp.where(first[:32], moved, packed)], axis=0
    )
    turned = jnp.concatenate([mixed, mixed], axis=0).T[:R]
    diag_g = total[0:1]
    moved = swap_halves(diag_g)
    diag_g = jnp.where(first[:1], diag_g, moved) + jnp.where(first[:1], moved, diag_g) * (1.0 / 1024.0)
    factor_a = jnp.where(col >= row, mixed, turned)
    factor_g = jnp.where(col < row, mixed, jnp.where(col > row, turned, diag_g))
    m = jnp.where(first, factor_a, factor_g) * (1.0 / tokens)
    on_diag = row == col
    diag = jnp.sum(jnp.where(on_diag, m, 0.0), axis=0, keepdims=True)
    trace_a = jnp.sum(jnp.where(first[:1], diag, 0.0), axis=1, keepdims=True)
    trace_g = jnp.sum(jnp.where(first[:1], 0.0, diag), axis=1, keepdims=True)
    damp = (DAMP / R) * jnp.where(first[:1], trace_a, trace_g) + 1e-06
    power_a = exponent(trace_a + R * damp[:, :1])
    power_g = exponent(trace_g + R * damp[:, R : R + 1])
    power_ref[...] = jnp.broadcast_to(power_a + power_g, (8, LANES))
    shrink = jnp.exp2(-jnp.where(first[:1], power_a, power_g))
    m = invert_pair(jnp.where(on_diag, m + damp, m) * shrink)
    other = swap_halves(m)
    ah, al = split(block_diagonal(jnp.where(first, m, other)))
    ig = jnp.where(first, other, m)[:, :R]
    g0 = ig.astype(BF16)
    g1, g2 = split(ig - g0.astype(F32))
    left = jnp.concatenate([g0, g1, g2], axis=0)
    left_ref[...] = left
    ah_ref[...] = ah
    al_ref[...] = al
    precondition(t_ref, left, ah, al, lh, ll, u, tp_ref)


def solve(parts, wide, tokens):
    vmem = pl.BlockSpec(memory_space=pltpu.VMEM)
    return pl.pallas_call(
        lambda *refs: solve_kernel(float(tokens), *refs),
        out_shape=(
            jax.ShapeDtypeStruct((Z * E_DEV, D), BF16),
            jax.ShapeDtypeStruct((3 * R, R), BF16),
            jax.ShapeDtypeStruct((4 * R, 4 * R), BF16),
            jax.ShapeDtypeStruct((4 * R, 4 * R), BF16),
            jax.ShapeDtypeStruct((8, LANES), F32),
        ),
        in_specs=[vmem] * (Y + 1),
        out_specs=(vmem,) * 5,
        scratch_shapes=[
            pltpu.VMEM((Z * R, 256), BF16),
            pltpu.VMEM((Z * R, 256), BF16),
            pltpu.VMEM((2 * Z * R, LANES), F32),
        ],
        compiler_params=pltpu.CompilerParams(vmem_limit_bytes=32 * MIB),
        cost_estimate=pl.CostEstimate(flops=4 * 10**9, bytes_accessed=2 * MIB, transcendentals=0),
        name="solve",
    )(*parts, wide)


def score_kernel(
    scale, tp, left_ref, ah_ref, al_ref, power_ref, wide, far, at_ref, q0, q1, out_ref, lh, ll, u, tq, names
):
    my_z, my_y, far_y = at_ref[0], at_ref[1], at_ref[2]
    precondition(far, left_ref[...], ah_ref[...], al_ref[...], lh, ll, u, tq)
    lanes = lane_iota(2 * Z)
    rows = row_iota(2 * Z)
    source = jnp.where(rows < Z, my_y, far_y)
    mine = (lanes // (Y * E_DEV) == rows % Z) & (lanes // E_DEV % Y == source)
    power = jnp.zeros((1, LANES), F32)
    listed = []
    for ref in (wide, far):
        for z in range(Z):
            power = power + ref[z, NOTES + 3 : NOTES + 4, :]
            listed.append(ref[z, NOTES + 4 : NOTES + 5, :])
    listed = jnp.concatenate(listed, axis=0).astype(BF16)
    names[...] = dot(listed, jnp.where(mine, 1.0, 0.0).astype(BF16), TN)
    named = names[pl.ds(pl.multiple_of(my_z * (Y * CAP), Y * CAP), Y * CAP), :]
    column = jnp.exp2(power - power_ref[0:1, :]) * scale

    examples = jnp.concatenate([tp[...], tq[...]], axis=0)
    s = jnp.concatenate([dot(q0[...], examples, NT), dot(q1[...], examples, NT)], axis=0)
    take = row_iota(64)
    y = jnp.where(take < 32, my_y, far_y)
    take = take % 32
    place = take % 16 // 2 * (Y * E_DEV) + y * E_DEV + take % 2 * 2 + take // 16
    onehot = jnp.where(place == lane_iota(64), 1.0, 0.0).astype(BF16)
    s0 = s.astype(BF16)
    s1, s2 = split(s - s0.astype(F32))
    s = dot(jnp.concatenate([s0, s1, s2], axis=0), onehot, NN)
    s = s[: 2 * R] + (s[2 * R : 4 * R] + s[4 * R :])
    blocks = (row_iota(R) // QB).astype(F32)
    for k in range(2):
        owner = my_y if k == 0 else my_y + 1 - my_y % 2 * 2
        id0, id1 = named[0:1], named[1:2]
        for y in range(1, Y):
            id0 = jnp.where(owner == y, named[2 * y : 2 * y + 1], id0)
            id1 = jnp.where(owner == y, named[2 * y + 1 : 2 * y + 2], id1)
        live = (blocks == id0) | (blocks == id1)
        out_ref[owner % 2] = jnp.where(live, s[k * R : (k + 1) * R] * column, 0.0)


def score(solved, wide, far, at, queries, scale):
    vmem = pl.BlockSpec(memory_space=pltpu.VMEM)
    smem = pl.BlockSpec(memory_space=pltpu.SMEM)
    return pl.pallas_call(
        lambda *refs: score_kernel(scale, *refs),
        out_shape=jax.ShapeDtypeStruct((2, R, LANES), F32),
        in_specs=[vmem] * 7 + [smem] + [vmem] * 2,
        out_specs=vmem,
        scratch_shapes=[
            pltpu.VMEM((Z * R, 256), BF16),
            pltpu.VMEM((Z * R, 256), BF16),
            pltpu.VMEM((2 * Z * R, LANES), F32),
            pltpu.VMEM((Z * E_DEV, D), BF16),
            pltpu.VMEM((LANES, LANES), F32),
        ],
        compiler_params=pltpu.CompilerParams(vmem_limit_bytes=32 * MIB),
        cost_estimate=pl.CostEstimate(flops=10**9, bytes_accessed=3 * MIB, transcendentals=0),
        name="score",
    )(*solved, wide, far, at, *queries)


def body(x_act, g_out, proj_in, proj_out, queries, cand_ids, cand_counts):
    n_layers = lax.axis_size("block")
    my_z = lax.axis_index("z").astype(jnp.int32)
    my_y = lax.axis_index(("yh", "yl")).astype(jnp.int32)
    me = my_z * Y + my_y
    far_y = (my_y + 3 + my_y % 2 * 2) % Y
    near = lax.ppermute(queries[0], "yl", [(0, 1), (1, 0)])
    packet = project(
        x_act[0],
        g_out[0],
        proj_in[0].T,
        proj_out[0].T,
        jnp.reshape(me, (1,)),
        cand_ids[0].T,
        cand_counts,
    )
    packet = jnp.broadcast_to(packet.astype(F16)[None], (Z, PACK, LANES))
    got = lax.all_to_all(packet, "z", 0, 0, tiled=True)

    r = jnp.arange(LOW - NOTES)[:, None] - (HIGH - NOTES)
    lane = jnp.arange(LANES)[None, :]
    upper = (lane % R >= r + R // 2 * (lane // R)) & (r >= 0)
    power = jnp.where(
        upper[None],
        got[:, NOTES + 1 : NOTES + 2].astype(F32),
        got[:, NOTES + 2 : NOTES + 3].astype(F32),
    )
    low = jnp.pad(got[:, LOW:].astype(F32), ((0, 0), (HIGH - NOTES, 0), (0, 0)))
    both = got[:, NOTES:LOW].astype(F32) + low * (1.0 / 1024.0)
    sums = jnp.sum(both * (jnp.exp2(power) * (1.0 / 128.0)), axis=0)
    parts = [sums] + [
        lax.ppermute(sums, ("yh", "yl"), [(y, (y + k) % Y) for y in range(Y)]) for k in range(1, Y)
    ]
    sums, got = lax.optimization_barrier((sums, got))
    own = got[:, :HIGH]
    far = lax.ppermute(own, ("yh", "yl"), [(0, 3), (3, 0), (1, 2), (2, 1)])

    scale = 1.0 / float(R * R * n_layers) ** 0.5 / 4096.0
    wide = own.astype(F32)
    solved = solve(parts, wide, ROWS * Z * Y)
    at = jnp.stack([my_z, my_y, far_y])
    scores = score(solved, wide, far.astype(F32), at, [queries[0], near], scale)
    scores = scores.reshape(2 * n_layers, R // n_layers, LANES)
    return jnp.sum(lax.all_to_all(scores, ("yl", "block"), 0, 0, tiled=True), axis=0)


def solution(mesh):
    axes = ("z", "yh", "yl", "block")
    split_mesh = Mesh(mesh.devices.reshape(Z, 2, 2, -1), axes)
    shard = axes[:3]
    return jax.shard_map(
        body,
        mesh=split_mesh,
        in_specs=(
            P("block", shard, None),
            P("block", shard, None),
            P("block", None, None),
            P("block", None, None),
            P("block", shard, None),
            P(shard, None, None),
            P(shard, None),
        ),
        out_specs=P(axes, None),
        check_vma=False,
    )
```
